256 devices in a mesh: row: 32 (over y, x, core), col: 8 (over z).
Axes of the slice: x: 4, y: 4, z: 8, core: 2. Of those that a mesh axis runs over, the one named last changes fastest.
Arguments:
- retarded: bfloat16 [256, 256, 64, 128], P('row', 'col'), may hold values from -4 to 4
- mirrored: bfloat16 [256, 256, 64, 128], P('col', 'row'), may hold values from -4 to 4
- lesser_panel: bfloat16 [256, 64, 16, 128], P(('col', 'row')), may hold values from -6 to 6
- initial: float32 [64, 16, 128], P(None, 'col'), may hold values from -6 to 6
- retention: float32 [256, 64], P('row'), may hold values from 0.4 to 1, as said below
- phase_angle: float32 [64], replicated, may hold values from -3.140625 to 3.140625
Outputs:
- propagated: float32 [256, 64, 16, 128], P('row', None, 'col')
The draws below stay inside these ranges and needn't reach their ends.
Inputs may be any that keep to these rules, and one draw needn't show every extreme that they name: `retention`: each entry is the share of an orbital's amplitude kept over one step.
All inputs are finite; a program needn't handle non-finite values.
Results may differ from the reference program's by a relative error of at most 0.0026.
Values may be sent and summed in bfloat16 or wider, within the bound.
No kernel may reach another device: no remote copies, remote signals or barrier semaphores. Data moves between devices by JAX's collectives and lax.ppermute only.
A program may use at most 128 MiB of HBM per device.

```python
import math
import jax
import jax.numpy as jnp
from jax import lax

ORBITAL_COUNT = 64
P_SIZE = 16
WINDOW_STEPS = 256


def draw_retention(key, part):
    child_random_keys = jax.random.split(jax.random.fold_in(key, 11), 5)
    ranking = jax.random.permutation(child_random_keys[0], ORBITAL_COUNT)
    slow_count = ORBITAL_COUNT // 2
    slow_mask = ranking < slow_count
    spread = jax.random.uniform(child_random_keys[1], (ORBITAL_COUNT,), jnp.float32)
    slow_rate = jnp.exp(jnp.log(0.05 / WINDOW_STEPS) + spread * (jnp.log(0.7 / WINDOW_STEPS) - jnp.log(0.05 / WINDOW_STEPS)))
    fast_rate = jnp.exp(jnp.log(1.0 / 50.0) + spread * (jnp.log(1.0 / 20.0) - jnp.log(1.0 / 50.0)))
    base_rate = jnp.where(slow_mask, slow_rate, fast_rate)
    roughness = jnp.exp(jax.random.uniform(child_random_keys[2], (WINDOW_STEPS, ORBITAL_COUNT), jnp.float32, jnp.log(0.5), jnp.log(2.0)))
    retained_mask = jnp.exp(-base_rate[None, :] * roughness)
    surge_row_list = jax.random.randint(child_random_keys[3], (2,), 0, WINDOW_STEPS)
    time_labels = jnp.arange(WINDOW_STEPS, dtype=jnp.int32)
    surge_event = jnp.any(time_labels[:, None] == surge_row_list[None, :], axis=1)
    surge_decay = jax.random.uniform(child_random_keys[4], (WINDOW_STEPS, ORBITAL_COUNT), jnp.float32, 0.5, 0.8)
    return jnp.where(surge_event[:, None], retained_mask * surge_decay, retained_mask)


def level_of(key, dims, cuts, least, high):
    def one(position, shards_of):
        steps = jax.random.uniform(jax.random.fold_in(jax.random.fold_in(key, 6), position), (shards_of,), jnp.float32, least / len(cuts), high / len(cuts))
        return jnp.repeat(jnp.exp(steps), dims[position] // shards_of).reshape((-1,) + (1,) * (len(dims) - position - 1))

    loudness = one(*cuts[0])
    for cut in cuts[1:]:
        loudness = loudness * one(*cut)
    return loudness


def centred(stream_key, extent, scale, reach, cuts=(), kind=jnp.bfloat16):
    result = scale * jax.random.normal(stream_key, extent, jnp.float32)
    if cuts:
        result = result * level_of(stream_key, extent, cuts, -0.22, 0.18)
    return jnp.clip(result, -reach, reach).astype(kind)


def setup_inputs(seed: int = 0) -> dict:
    key_of = jax.random.split(jax.random.key(seed), 7)
    retarded = centred(key_of[0], (WINDOW_STEPS, WINDOW_STEPS, ORBITAL_COUNT, 2 * ORBITAL_COUNT), 0.7, 4.0, ((0, 32), (1, 8)))
    mirrored = centred(key_of[1], (WINDOW_STEPS, WINDOW_STEPS, ORBITAL_COUNT, 2 * ORBITAL_COUNT), 0.7, 4.0, ((0, 8), (1, 32)))
    lesser_panel = centred(key_of[2], (WINDOW_STEPS, ORBITAL_COUNT, P_SIZE, 2 * ORBITAL_COUNT), 1.0, 6.0, ((0, 256),))
    initial = centred(key_of[3], (ORBITAL_COUNT, P_SIZE, 2 * ORBITAL_COUNT), 1.0, 6.0, ((1, 8),), jnp.float32)
    retention = draw_retention(jax.random.fold_in(key_of[6], 71), 0)
    phase_angle = jnp.clip(jax.random.uniform(key_of[5], (ORBITAL_COUNT,), jnp.float32, -3.140625, 3.140625), -3.140625, 3.140625)
    return dict(retarded=retarded, mirrored=mirrored, lesser_panel=lesser_panel, initial=initial, retention=retention, phase_angle=phase_angle)


def complex_scale(scale_re, scale_im, current):
    orbit_count = current.shape[-1] // 2
    current_re = current[..., :orbit_count]
    current_im = current[..., orbit_count:]
    factor_re = scale_re[:, None, None]
    factor_im = scale_im[:, None, None]
    return jnp.concatenate([factor_re * current_re - factor_im * current_im, factor_re * current_im + factor_im * current_re], axis=-1)

def self_energy(retarded_tile, mirror_tile):
    orbit_count = retarded_tile.shape[-2]
    ret_re = retarded_tile[..., :orbit_count].astype(jnp.float32)
    ret_im = retarded_tile[..., orbit_count:].astype(jnp.float32)
    mirror_re = jnp.swapaxes(mirror_tile[..., :orbit_count], -1, -2).astype(jnp.float32)
    mirror_im = jnp.swapaxes(mirror_tile[..., orbit_count:], -1, -2).astype(jnp.float32)
    square_re = ret_re * ret_re - ret_im * ret_im
    square_im = 2.0 * ret_re * ret_im
    return jnp.concatenate([square_re * mirror_re - square_im * mirror_im, square_re * mirror_im + square_im * mirror_re], axis=-1)

def reference(retarded, mirrored, lesser_panel, initial, retention, phase_angle):
    panel_matrix = lesser_panel.reshape(WINDOW_STEPS * ORBITAL_COUNT, P_SIZE * 2 * ORBITAL_COUNT)
    norm_factor = 1.0 / (ORBITAL_COUNT * math.sqrt(WINDOW_STEPS))
    positions = jnp.arange(WINDOW_STEPS, dtype=jnp.int32)

    def one_time(time_index):
        row_tiles = retarded[time_index]
        mirror_tiles = mirrored[:, time_index]
        energy = self_energy(row_tiles, mirror_tiles)
        energy = jnp.where((positions <= time_index)[:, None, None], energy, 0.0).astype(jnp.bfloat16)
        energy_re = jnp.transpose(energy[..., :ORBITAL_COUNT], (1, 0, 2)).reshape(ORBITAL_COUNT, WINDOW_STEPS * ORBITAL_COUNT)
        energy_im = jnp.transpose(energy[..., ORBITAL_COUNT:], (1, 0, 2)).reshape(ORBITAL_COUNT, WINDOW_STEPS * ORBITAL_COUNT)
        stacked = jnp.concatenate([energy_re, energy_im], axis=0)
        product = jnp.dot(stacked, panel_matrix, preferred_element_type=jnp.float32).reshape(2, ORBITAL_COUNT, P_SIZE, 2, ORBITAL_COUNT)
        integral_re = product[0, :, :, 0] - product[1, :, :, 1]
        integral_im = product[0, :, :, 1] + product[1, :, :, 0]
        return jnp.concatenate([integral_re, integral_im], axis=-1) * norm_factor
    integrals = lax.map(one_time, jnp.arange(WINDOW_STEPS, dtype=jnp.int32))
    rotate_re = retention * jnp.cos(phase_angle)[None, :]
    rotate_im = retention * jnp.sin(phase_angle)[None, :]

    def advance(current, inputs):
        scale_re, scale_im, integral = inputs
        updated = complex_scale(scale_re, scale_im, current + integral)
        return (updated, updated)
    last_state, states = lax.scan(advance, initial, (rotate_re, rotate_im, integrals))
    return states
```

```python
import math

import jax
import jax.numpy as jnp
from jax import lax
from jax.experimental import pallas as pl
from jax.experimental.pallas import tpu as pltpu
from jax.sharding import PartitionSpec as P


Y, X, CORES, Z = 4, 4, 2, 8
OFFSETS = (0, -1, 1, 2)
BOTH = ("row", "col")


def joint(y, x, core, z):
    return (((y % Y) * X + (x % X)) * CORES + core) * Z + z % Z


def perm_of(target):
    pairs = []
    for y in range(Y):
        for x in range(X):
            for core in range(CORES):
                for z in range(Z):
                    pairs.append((joint(y, x, core, z), joint(*target(y, x, core, z))))
    return pairs


def plane_perm(by, first):
    return perm_of(
        lambda y, x, core, z: (y, x + by, core, z)
        if (core == 0) == first
        else (y + by, x, core, z)
    )


def depth_perm(by):
    return perm_of(lambda y, x, core, z: (y, x, core, z + (by if core == 0 else -by)))


CORE_SWAP = perm_of(lambda y, x, core, z: (y, x, 1 - core, z))


def send(array, perm):
    return lax.ppermute(array, BOTH, perm)


def energy_kernel(slots, times, ret_ref, mir_ref, out_ref):
    orbitals = ret_ref.shape[2]
    slot_count = ret_ref.shape[1]
    now = times[0] + pl.program_id(0)
    first_source = times[1]
    low = lax.broadcasted_iota(jnp.int32, (orbitals, 2 * orbitals), 1) < orbitals
    low_row = lax.broadcasted_iota(jnp.int32, (1, 2 * orbitals), 1) < orbitals

    def pair(n, carry):
        s0 = slots[2 * n]
        s1 = slots[2 * n + 1]
        a0 = ret_ref[0, s0].astype(jnp.float32)
        a1 = ret_ref[0, s1].astype(jnp.float32)
        b = jnp.concatenate([mir_ref[s0, 0], mir_ref[s1, 0]], axis=0).astype(jnp.float32)
        keep0 = jnp.where(first_source + s0 <= now, 1.0, 0.0)
        keep1 = jnp.where(first_source + s1 <= now, 1.0, 0.0)
        keep = jnp.where(low_row, keep0, keep1)
        bt = b.T
        b_re = bt[:orbitals] * keep
        b_im = bt[orbitals:] * keep
        re = jnp.where(low, a0, pltpu.roll(a1, orbitals, 1))
        im = jnp.where(low, pltpu.roll(a0, orbitals, 1), a1)
        sq_re = re * re - im * im
        sq_im = 2.0 * re * im
        cols = pl.ds(pl.multiple_of(n * 2 * orbitals, 2 * orbitals), 2 * orbitals)
        out_ref[0, 0, :, cols] = (sq_re * b_re - sq_im * b_im).astype(jnp.bfloat16)
        out_ref[0, 1, :, cols] = (sq_re * b_im + sq_im * b_re).astype(jnp.bfloat16)
        return carry

    lax.fori_loop(0, slot_count // 2, pair, 0)


def energy_call(retarded, mirrored, slots, times):
    steps, sources, orbitals, width = retarded.shape
    return pl.pallas_call(
        energy_kernel,
        out_shape=jax.ShapeDtypeStruct((steps, 2, orbitals, sources * orbitals), jnp.bfloat16),
        grid_spec=pltpu.PrefetchScalarGridSpec(
            num_scalar_prefetch=2,
            grid=(steps,),
            in_specs=[
                pl.BlockSpec((1, sources, orbitals, width), lambda t, *_: (t, 0, 0, 0)),
                pl.BlockSpec((sources, 1, orbitals, width), lambda t, *_: (0, t, 0, 0)),
            ],
            out_specs=pl.BlockSpec(
                (1, 2, orbitals, sources * orbitals), lambda t, *_: (t, 0, 0, 0)
            ),
        ),
        compiler_params=pltpu.CompilerParams(vmem_limit_bytes=24 << 20),
        cost_estimate=pl.CostEstimate(
            flops=20 * steps * sources * orbitals * width,
            bytes_accessed=6 * steps * sources * orbitals * width,
            transcendentals=0,
        ),
    )(slots, times, retarded, mirrored)


def product_tile(energy_ref, panel_refs, norm):
    steps, _, orbitals, depth = energy_ref.shape
    width = 2 * orbitals
    left = energy_ref[...].reshape(steps * 2 * orbitals, depth)
    right = jnp.concatenate([ref[...] for ref in panel_refs], axis=0)
    both = jnp.dot(left, right, preferred_element_type=jnp.float32)
    both = both.reshape(steps, 2, orbitals, 2 * width)
    lane = lax.broadcasted_iota(jnp.int32, (steps, orbitals, width), 2)
    sign = jnp.where(lane < orbitals, -norm, norm)
    values = []
    for half in range(2):
        part_re = both[:, 0, :, half * width : (half + 1) * width]
        part_im = both[:, 1, :, half * width : (half + 1) * width]
        values.append(part_re * norm + sign * pltpu.roll(part_im, orbitals, 2))
    return values


def first_kernel(norm, cols, energy_ref, *refs):
    panel_refs, out_refs = refs[:8], refs[8:]
    values = product_tile(energy_ref, panel_refs, norm)
    for turn in range(2):

        @pl.when(pl.program_id(0) == turn)
        def _():
            for half in range(2):
                out_refs[2 * turn + half][...] = values[half].astype(jnp.bfloat16)


def rest_kernel(norm, cols, energy_ref, *refs):
    panel_refs, out_ref = refs[:8], refs[8]
    values = product_tile(energy_ref, panel_refs, norm)
    for half in range(2):
        out_ref[0, half] = values[half]


def product_specs(energy, panels, width):
    specs = [pl.BlockSpec(energy.shape, lambda n, cols: (0, 0, 0, 0), pipeline_mode=pl.Buffered(1))]
    for panel in panels:
        specs.append(pl.BlockSpec((panel.shape[0], 2 * width), lambda n, cols: (0, cols[n])))
    return specs


def product_call(kernel, norm, cols, energy, panels, tiles, split):
    steps, _, orbitals, depth = energy.shape
    width = 2 * orbitals
    if split:
        shape = [jax.ShapeDtypeStruct((steps, orbitals, width), jnp.bfloat16)] * 4
        out_specs = [pl.BlockSpec((steps, orbitals, width), lambda n, cols: (0, 0, 0))] * 4
    else:
        shape = jax.ShapeDtypeStruct((tiles, 2, steps, orbitals, width), jnp.float32)
        out_specs = pl.BlockSpec(
            (1, 2, steps, orbitals, width), lambda n, cols: (n, 0, 0, 0, 0)
        )

    def body(cols_ref, *refs):
        kernel(norm, cols_ref, *refs)

    return pl.pallas_call(
        body,
        out_shape=shape,
        grid_spec=pltpu.PrefetchScalarGridSpec(
            num_scalar_prefetch=1,
            grid=(tiles,),
            in_specs=product_specs(energy, panels, width),
            out_specs=out_specs,
        ),
        compiler_params=pltpu.CompilerParams(vmem_limit_bytes=32 << 20),
        cost_estimate=pl.CostEstimate(
            flops=2 * tiles * steps * 2 * orbitals * depth * 2 * width,
            bytes_accessed=2 * depth * (steps * 2 * orbitals + tiles * 2 * width),
            transcendentals=0,
        ),
    )(cols, energy, *panels)


def turned(factor_re, factor_im, value):
    return factor_re * value + factor_im * pltpu.roll(value, value.shape[-1] // 2, value.ndim - 1)


def end_kernel(fre_ref, fim_ref, own_ref, fa_ref, fb_ref, ba_ref, bb_ref, sum_ref, msg_ref):
    steps, orbitals, width = fa_ref.shape
    lane = lax.broadcasted_iota(jnp.int32, (orbitals, width), 1)
    block = jnp.where(lane < width // 2, 1.0, 0.0).astype(jnp.float32)
    for half, (f_ref, b_ref) in enumerate(((fa_ref, ba_ref), (fb_ref, bb_ref))):
        state = jnp.zeros((orbitals, width), jnp.float32)
        for t in range(steps):
            value = f_ref[t].astype(jnp.float32) + b_ref[t].astype(jnp.float32) + own_ref[half, t]
            sum_ref[half, t] = value
            state = turned(fre_ref[t], fim_ref[t], state + value)
        msg_ref[half] = state
    for t in range(steps):
        block = turned(fre_ref[t], fim_ref[t], block)
    msg_ref[2] = block


def apply(later, earlier):
    width = later.shape[-1]
    lane = lax.broadcasted_iota(jnp.int32, later.shape[1:], 1)
    low = lane < width // 2
    factor = later[2]
    swapped = pltpu.roll(factor, width // 2, 1)
    fre = jnp.where(low, factor, swapped)
    fim = jnp.where(low, -swapped, factor)
    planes = [
        turned(fre, fim, earlier[0]) + later[0],
        turned(fre, fim, earlier[1]) + later[1],
        turned(fre, fim, earlier[2]),
    ]
    return planes


def chosen(keep, planes, other):
    return [jnp.where(keep, a, b) for a, b in zip(planes, other)]


def unit(shape):
    lane = lax.broadcasted_iota(jnp.int32, shape, 1)
    return [
        jnp.zeros(shape, jnp.float32),
        jnp.zeros(shape, jnp.float32),
        jnp.where(lane < shape[-1] // 2, 1.0, 0.0).astype(jnp.float32),
    ]


def read(ref):
    return [ref[0], ref[1], ref[2]]


class Planes:
    def __init__(self, planes):
        self.planes = planes
        self.shape = (3,) + planes[0].shape

    def __getitem__(self, index):
        return self.planes[index]


def after(later, earlier):
    return apply(Planes(later), Planes(earlier))


def chip_kernel(where_ref, own_ref, other_ref, out_ref):
    odd = where_ref[0] == 1
    own, other = read(own_ref), read(other_ref)
    later = chosen(odd, own, other)
    earlier = chosen(odd, other, own)
    for n, plane in enumerate(after(later, earlier)):
        out_ref[n] = plane


def line_kernel(place, where_ref, own_ref, d1_ref, d2_ref, d3_ref, before_ref, total_ref):
    at = where_ref[place]
    one = unit(own_ref.shape[1:])
    behind = [read(d1_ref), read(d2_ref), read(d3_ref)]
    before = one
    for back in (3, 2, 1):
        here = chosen(at >= back, behind[back - 1], one)
        before = after(here, before)
    for n, plane in enumerate(before):
        before_ref[n] = plane
    if total_ref is not None:
        total = after(read(own_ref), before)
        for back in (3, 2, 1):
            here = chosen(at < back, behind[back - 1], one)
            total = after(here, total)
        for n, plane in enumerate(total):
            total_ref[n] = plane


def column_kernel(where_ref, own_ref, d1_ref, d2_ref, d3_ref, before_ref):
    line_kernel(2, where_ref, own_ref, d1_ref, d2_ref, d3_ref, before_ref, None)


def last_kernel(where_ref, fre_ref, fim_ref, sum_ref, init_ref, y_ref, x_ref, core_ref, out_ref):
    steps = fre_ref.shape[0]
    one = unit(init_ref.shape[1:])
    from_core = chosen(where_ref[0] == 1, read(core_ref), one)
    entering = after(from_core, after(read(x_ref), read(y_ref)))
    start = after(entering, [init_ref[0], init_ref[1], one[2]])
    for half in range(2):
        state = start[half]
        for t in range(steps):
            state = turned(fre_ref[t], fim_ref[t], state + sum_ref[half, t])
            out_ref[t, half] = state


def small_call(kernel, out_shape, scalars, *arrays):
    specs = [pl.BlockSpec(memory_space=pltpu.SMEM)] if scalars is not None else []
    specs += [pl.BlockSpec(memory_space=pltpu.VMEM)] * len(arrays)
    out_specs = jax.tree.map(lambda _: pl.BlockSpec(memory_space=pltpu.VMEM), out_shape)
    args = ([scalars] if scalars is not None else []) + list(arrays)
    return pl.pallas_call(
        kernel,
        out_shape=out_shape,
        in_specs=specs,
        out_specs=out_specs,
        compiler_params=pltpu.CompilerParams(vmem_limit_bytes=16 << 20),
        cost_estimate=pl.CostEstimate(flops=1000000, bytes_accessed=1 << 20, transcendentals=0),
    )(*args)


def gather_panel(local):
    moved = [local] + [send(local, plane_perm(-off, True)) for off in OFFSETS[1:]]
    line = jnp.concatenate(moved, axis=0)
    blocks = [line] + [send(line, plane_perm(-off, False)) for off in OFFSETS[1:]]
    return blocks + [send(block, CORE_SWAP) for block in blocks]


def slot_table(row_index):
    core = row_index % CORES
    x = (row_index // CORES) % X
    y = row_index // (CORES * X)
    offs = jnp.array(OFFSETS, jnp.int32)
    outer = jnp.repeat(offs, len(OFFSETS))
    inner = jnp.tile(offs, len(OFFSETS))

    def of(which):
        dy = jnp.where(which == 0, outer, inner)
        dx = jnp.where(which == 0, inner, outer)
        return (((y + dy) % Y) * X + (x + dx) % X) * CORES + which

    return jnp.concatenate([of(core), of(1 - core)]).astype(jnp.int32)


def per_device(retarded, mirrored, lesser_panel, initial, retention, phase_angle):
    row_index = lax.axis_index("row")
    col_index = lax.axis_index("col")
    steps, sources, orbitals, width = retarded.shape
    window = steps * lax.axis_size("row")
    panels = lesser_panel.shape[2]
    norm = 1.0 / (orbitals * math.sqrt(window))
    core = row_index % CORES
    x = (row_index // CORES) % X
    y = row_index // (CORES * X)
    where = jnp.stack([core, x, y]).astype(jnp.int32)
    way = jnp.where(core == 0, 1, -1)

    local = lesser_panel.reshape(orbitals, panels * width)
    blocks = gather_panel(local)

    times = jnp.stack([row_index * steps, col_index * sources]).astype(jnp.int32)
    energy = energy_call(retarded, mirrored, slot_table(row_index), times)

    def cols_of(rels):
        return ((col_index + way * jnp.array(rels, jnp.int32)) % Z).astype(jnp.int32)

    f0, f1, b0, b1 = product_call(
        first_kernel, norm, cols_of((4, 5)), energy, blocks, 2, True
    )
    order = (3, 6, 2, 7, 1, 0)
    rest = product_call(rest_kernel, norm, cols_of(order), energy, blocks, len(order), False)

    forward, backward = [f0, f1], [b0, b1]
    for rel in (3, 2, 1):
        for half in range(2):
            got = send(forward[half], depth_perm(1)).astype(jnp.float32)
            forward[half] = (got + rest[order.index(rel), half]).astype(jnp.bfloat16)
    for rel in (6, 7):
        for half in range(2):
            got = send(backward[half], depth_perm(-1)).astype(jnp.float32)
            backward[half] = (got + rest[order.index(rel), half]).astype(jnp.bfloat16)
    forward = [send(v, depth_perm(1)) for v in forward]
    backward = [send(v, depth_perm(-1)) for v in backward]

    rotate_re = retention * jnp.cos(phase_angle)[None, :]
    rotate_im = retention * jnp.sin(phase_angle)[None, :]
    lane = jnp.arange(width, dtype=jnp.int32)
    sign = jnp.where(lane < orbitals, -1.0, 1.0).astype(jnp.float32)
    fre = jnp.broadcast_to(rotate_re[:, :, None], (steps, orbitals, width))
    fim = rotate_im[:, :, None] * sign
    start = jnp.swapaxes(initial, 0, 1)

    message = jax.ShapeDtypeStruct((3, orbitals, width), jnp.float32)
    total = jax.ShapeDtypeStruct((2, steps, orbitals, width), jnp.float32)
    own = rest[order.index(0)]
    summed, ends = small_call(
        end_kernel, (total, message), None, fre, fim, own, *forward, *backward
    )
    other = send(ends, CORE_SWAP)
    chip = small_call(chip_kernel, message, where, ends, other)
    row_perm = lambda by: perm_of(lambda y, x, core, z: (y, x + by, core, z))
    column_perm = lambda by: perm_of(lambda y, x, core, z: (y + by, x, core, z))
    behind = [send(chip, row_perm(back)) for back in (1, 2, 3)]

    def across(*refs):
        line_kernel(1, *refs)

    before_x, line = small_call(across, (message, message), where, chip, *behind)
    behind = [send(line, column_perm(back)) for back in (1, 2, 3)]
    before_y = small_call(column_kernel, message, where, line, *behind)
    out = small_call(
        last_kernel,
        jax.ShapeDtypeStruct((steps, 2, orbitals, width), jnp.float32),
        where,
        fre,
        fim,
        summed,
        start,
        before_y,
        before_x,
        other,
    )
    return jnp.swapaxes(out, 1, 2)


def solution(mesh):
    return jax.shard_map(
        per_device,
        mesh=mesh,
        in_specs=(
            P("row", "col", None, None),
            P("col", "row", None, None),
            P(("col", "row"), None, None, None),
            P(None, "col", None),
            P("row", None),
            P(),
        ),
        out_specs=P("row", None, "col", None),
        check_vma=False,
    )
```

```python
import math

import jax
import jax.numpy as jnp
from jax import lax
from jax.experimental import pallas as pl
from jax.experimental.pallas import tpu as pltpu
from jax.sharding import PartitionSpec as P


Y, X, CORES, Z = 4, 4, 2, 8
OFFSETS = (0, -1, 1, 2)
BOTH = ("row", "col")


def joint(y, x, core, z):
    return (((y % Y) * X + (x % X)) * CORES + core) * Z + z % Z


def perm_of(target):
    pairs = []
    for y in range(Y):
        for x in range(X):
            for core in range(CORES):
                for z in range(Z):
                    pairs.append((joint(y, x, core, z), joint(*target(y, x, core, z))))
    return pairs


def plane_perm(by, first):
    return perm_of(
        lambda y, x, core, z: (y, x + by, core, z)
        if (core == 0) == first
        else (y + by, x, core, z)
    )


def depth_perm(by):
    return perm_of(lambda y, x, core, z: (y, x, core, z + (by if core == 0 else -by)))


CORE_SWAP = perm_of(lambda y, x, core, z: (y, x, 1 - core, z))


def send(array, perm):
    return lax.ppermute(array, BOTH, perm)


def energy_kernel(slots, times, ret_ref, mir_ref, out_ref):
    orbitals = ret_ref.shape[2]
    slot_count = ret_ref.shape[1]
    now = times[0] + pl.program_id(0)
    first_source = times[1]
    low = lax.broadcasted_iota(jnp.int32, (orbitals, 2 * orbitals), 1) < orbitals
    low_row = lax.broadcasted_iota(jnp.int32, (1, 2 * orbitals), 1) < orbitals

    def pair(n, carry):
        s0 = slots[2 * n]
        s1 = slots[2 * n + 1]
        a0 = ret_ref[0, s0].astype(jnp.float32)
        a1 = ret_ref[0, s1].astype(jnp.float32)
        b = jnp.concatenate([mir_ref[s0, 0], mir_ref[s1, 0]], axis=0).astype(jnp.float32)
        keep0 = jnp.where(first_source + s0 <= now, 1.0, 0.0)
        keep1 = jnp.where(first_source + s1 <= now, 1.0, 0.0)
        keep = jnp.where(low_row, keep0, keep1)
        bt = b.T
        b_re = bt[:orbitals] * keep
        b_im = bt[orbitals:] * keep
        re = jnp.where(low, a0, pltpu.roll(a1, orbitals, 1))
        im = jnp.where(low, pltpu.roll(a0, orbitals, 1), a1)
        sq_re = re * re - im * im
        sq_im = 2.0 * re * im
        cols = pl.ds(pl.multiple_of(n * 2 * orbitals, 2 * orbitals), 2 * orbitals)
        out_ref[pl.program_id(0), 0, :, cols] = (sq_re * b_re - sq_im * b_im).astype(jnp.bfloat16)
        out_ref[pl.program_id(0), 1, :, cols] = (sq_re * b_im + sq_im * b_re).astype(jnp.bfloat16)
        return carry

    lax.fori_loop(0, slot_count // 2, pair, 0, unroll=4)


def energy_call(retarded, mirrored, slots, times):
    steps, sources, orbitals, width = retarded.shape
    return pl.pallas_call(
        energy_kernel,
        out_shape=jax.ShapeDtypeStruct((steps, 2, orbitals, sources * orbitals), jnp.bfloat16),
        grid_spec=pltpu.PrefetchScalarGridSpec(
            num_scalar_prefetch=2,
            grid=(steps,),
            in_specs=[
                pl.BlockSpec((1, sources, orbitals, width), lambda t, *_: (t, 0, 0, 0)),
                pl.BlockSpec((sources, 1, orbitals, width), lambda t, *_: (0, t, 0, 0)),
            ],
            out_specs=pl.BlockSpec(memory_space=pltpu.VMEM),
        ),
        compiler_params=pltpu.CompilerParams(vmem_limit_bytes=14 << 20),
        cost_estimate=pl.CostEstimate(
            flops=20 * steps * sources * orbitals * width,
            bytes_accessed=6 * steps * sources * orbitals * width,
            transcendentals=0,
        ),
    )(
        slots,
        times,
        pltpu.with_memory_space_constraint(retarded, pltpu.HBM),
        pltpu.with_memory_space_constraint(mirrored, pltpu.HBM),
    )


def product_tile(energy_ref, panel_refs, norm):
    steps, _, orbitals, depth = energy_ref.shape
    width = 2 * orbitals
    left = energy_ref[...].reshape(steps * 2 * orbitals, depth)
    count = len(panel_refs) // 2
    right = jnp.concatenate(
        [
            jnp.concatenate([ref[...] for ref in panel_refs[:count]], axis=0),
            jnp.concatenate([ref[...] for ref in panel_refs[count:]], axis=0),
        ],
        axis=1,
    )
    both = jnp.dot(left, right, preferred_element_type=jnp.float32)
    both = both.reshape(steps, 2, orbitals, 2 * width)
    lane = lax.broadcasted_iota(jnp.int32, (steps, orbitals, width), 2)
    sign = jnp.where(lane < orbitals, -norm, norm)
    values = []
    for half in range(2):
        part_re = both[:, 0, :, half * width : (half + 1) * width]
        part_im = both[:, 1, :, half * width : (half + 1) * width]
        values.append(part_re * norm + sign * pltpu.roll(part_im, orbitals, 2))
    return values


def product_call(norm, cols, energy, panels, outputs):
    steps, _, orbitals, depth = energy.shape
    width = 2 * orbitals
    sizes, kinds = {}, {}
    for turn in outputs:
        for result, place, kind in turn:
            sizes[result] = max(sizes.get(result, 0), place + 1)
            kinds[result] = kind
    shape = [
        jax.ShapeDtypeStruct((sizes[n], steps, orbitals, width), kinds[n]) for n in range(len(sizes))
    ]
    count = len(panels)

    def body(cols_ref, energy_ref, *refs):
        panel_refs, out_refs = refs[: 2 * count], refs[2 * count :]
        values = product_tile(energy_ref, panel_refs, norm)
        for turn, targets in enumerate(outputs):

            @pl.when(pl.program_id(0) == turn)
            def _():
                for value, (result, place, kind) in zip(values, targets):
                    out_refs[result][place] = value.astype(kind)

    def panel_spec(panel, which):
        return pl.BlockSpec((panel.shape[0], width), lambda n, cols: (0, cols[2 * n + which]))

    return pl.pallas_call(
        body,
        out_shape=shape,
        grid_spec=pltpu.PrefetchScalarGridSpec(
            num_scalar_prefetch=1,
            grid=(len(outputs),),
            in_specs=[pl.BlockSpec(memory_space=pltpu.VMEM)]
            + [panel_spec(panel, which) for which in range(2) for panel in panels],
            out_specs=[pl.BlockSpec(s.shape, lambda n, cols: (0, 0, 0, 0)) for s in shape],
        ),
        compiler_params=pltpu.CompilerParams(vmem_limit_bytes=20 << 20),
        cost_estimate=pl.CostEstimate(
            flops=2 * len(outputs) * steps * 2 * orbitals * depth * 2 * width,
            bytes_accessed=2 * depth * (steps * 2 * orbitals + len(outputs) * 2 * width),
            transcendentals=0,
        ),
    )(cols, energy, *panels, *panels)


def turned(factor_re, factor_im, value):
    return factor_re * value + factor_im * pltpu.roll(value, value.shape[-1] // 2, value.ndim - 1)


def end_kernel(fre_ref, fim_ref, *refs):
    part_refs, (sum_ref, end_ref) = refs[:-2], refs[-2:]
    steps, orbitals, width = sum_ref.shape
    state = jnp.zeros((orbitals, width), jnp.float32)
    for t in range(steps):
        value = part_refs[0][t]
        for ref in part_refs[1:]:
            value = value + ref[t].astype(jnp.float32)
        sum_ref[t] = value
        state = turned(fre_ref[t], fim_ref[t], state + value)
    end_ref[...] = state


def message_kernel(fre_ref, fim_ref, end0_ref, end1_ref, msg_ref):
    steps, orbitals, width = fre_ref.shape
    lane = lax.broadcasted_iota(jnp.int32, (orbitals, width), 1)
    block = jnp.where(lane < width // 2, 1.0, 0.0).astype(jnp.float32)
    for t in range(steps):
        block = turned(fre_ref[t], fim_ref[t], block)
    msg_ref[0] = end0_ref[...]
    msg_ref[1] = end1_ref[...]
    msg_ref[2] = block


def apply(later, earlier):
    width = later.shape[-1]
    lane = lax.broadcasted_iota(jnp.int32, later.shape[1:], 1)
    low = lane < width // 2
    factor = later[2]
    swapped = pltpu.roll(factor, width // 2, 1)
    fre = jnp.where(low, factor, swapped)
    fim = jnp.where(low, -swapped, factor)
    planes = [
        turned(fre, fim, earlier[0]) + later[0],
        turned(fre, fim, earlier[1]) + later[1],
        turned(fre, fim, earlier[2]),
    ]
    return planes


def chosen(keep, planes, other):
    return [jnp.where(keep, a, b) for a, b in zip(planes, other)]


def unit(shape):
    lane = lax.broadcasted_iota(jnp.int32, shape, 1)
    return [
        jnp.zeros(shape, jnp.float32),
        jnp.zeros(shape, jnp.float32),
        jnp.where(lane < shape[-1] // 2, 1.0, 0.0).astype(jnp.float32),
    ]


def read(ref):
    return [ref[0], ref[1], ref[2]]


class Planes:
    def __init__(self, planes):
        self.planes = planes
        self.shape = (3,) + planes[0].shape

    def __getitem__(self, index):
        return self.planes[index]


def after(later, earlier):
    return apply(Planes(later), Planes(earlier))


def chip_kernel(where_ref, own_ref, other_ref, out_ref):
    odd = where_ref[0] == 1
    own, other = read(own_ref), read(other_ref)
    later = chosen(odd, own, other)
    earlier = chosen(odd, other, own)
    for n, plane in enumerate(after(later, earlier)):
        out_ref[n] = plane


def line_kernel(place, where_ref, own_ref, d1_ref, d2_ref, d3_ref, before_ref, total_ref):
    at = where_ref[place]
    one = unit(own_ref.shape[1:])
    behind = [read(d1_ref), read(d2_ref), read(d3_ref)]
    before = one
    for back in (3, 2, 1):
        here = chosen(at >= back, behind[back - 1], one)
        before = after(here, before)
    for n, plane in enumerate(before):
        before_ref[n] = plane
    if total_ref is not None:
        total = after(read(own_ref), before)
        for back in (3, 2, 1):
            here = chosen(at < back, behind[back - 1], one)
            total = after(here, total)
        for n, plane in enumerate(total):
            total_ref[n] = plane


def column_kernel(where_ref, own_ref, d1_ref, d2_ref, d3_ref, before_ref):
    line_kernel(2, where_ref, own_ref, d1_ref, d2_ref, d3_ref, before_ref, None)


def last_kernel(where_ref, fre_ref, fim_ref, sum0_ref, sum1_ref, init_ref, y_ref, x_ref, core_ref, out_ref):
    steps = fre_ref.shape[0]
    one = unit(init_ref.shape[1:])
    from_core = chosen(where_ref[0] == 1, read(core_ref), one)
    entering = after(from_core, after(read(x_ref), read(y_ref)))
    start = after(entering, [init_ref[0], init_ref[1], one[2]])
    for half, sum_ref in enumerate((sum0_ref, sum1_ref)):
        state = start[half]
        for t in range(steps):
            state = turned(fre_ref[t], fim_ref[t], state + sum_ref[t])
            out_ref[t, half] = state


def small_call(kernel, out_shape, scalars, *arrays):
    specs = [pl.BlockSpec(memory_space=pltpu.SMEM)] if scalars is not None else []
    specs += [pl.BlockSpec(memory_space=pltpu.VMEM)] * len(arrays)
    out_specs = jax.tree.map(lambda _: pl.BlockSpec(memory_space=pltpu.VMEM), out_shape)
    args = ([scalars] if scalars is not None else []) + list(arrays)
    return pl.pallas_call(
        kernel,
        out_shape=out_shape,
        in_specs=specs,
        out_specs=out_specs,
        compiler_params=pltpu.CompilerParams(vmem_limit_bytes=8 << 20),
        cost_estimate=pl.CostEstimate(flops=1000000, bytes_accessed=1 << 20, transcendentals=0),
    )(*args)


def near_line(local):
    moved = [local] + [send(local, plane_perm(-off, True)) for off in OFFSETS[1:]]
    return [jnp.concatenate([m[chunk] for m in moved], axis=0) for chunk in range(2)]


def far_blocks(line):
    blocks = [line]
    for off in OFFSETS[1:]:
        blocks.append(send(line, plane_perm(-off, False)))
    return blocks


def add_rounded(*parts):
    total = parts[0]
    for part in parts[1:]:
        total = total + part.astype(jnp.float32)
    return total.astype(jnp.bfloat16)


def column_sum(norm, cols_of, energy, panels):
    bf16, f32 = jnp.bfloat16, jnp.float32
    s46, s2, s7 = product_call(
        norm,
        cols_of((4, 6, 2, 7)),
        energy,
        panels,
        (((0, 0, bf16), (0, 1, bf16)), ((1, 0, bf16), (2, 0, bf16))),
    )
    r46 = send(s46, depth_perm(1))
    r2 = send(s2, depth_perm(-1))
    p3, p5, s1, p0 = product_call(
        norm,
        cols_of((3, 5, 1, 0)),
        energy,
        panels,
        (((0, 0, f32), (1, 0, f32)), ((2, 0, bf16), (3, 0, f32))),
    )
    r5 = send(add_rounded(p5[0], r46[1]), depth_perm(-3))
    r3 = send(add_rounded(p3[0], r46[0], r2[0]), depth_perm(3))
    r1 = send(s1[0], depth_perm(1))
    r7 = send(s7[0], depth_perm(-1))
    return [p0[0], r1, r7, r5, r3]


def slot_table(row_index):
    core = row_index % CORES
    x = (row_index // CORES) % X
    y = row_index // (CORES * X)
    offs = jnp.array(OFFSETS, jnp.int32)
    outer = jnp.repeat(offs, len(OFFSETS))
    inner = jnp.tile(offs, len(OFFSETS))

    def of(which):
        dy = jnp.where(which == 0, outer, inner)
        dx = jnp.where(which == 0, inner, outer)
        return (((y + dy) % Y) * X + (x + dx) % X) * CORES + which

    return jnp.concatenate([of(core), of(1 - core)]).astype(jnp.int32)


def per_device(retarded, mirrored, lesser_panel, initial, retention, phase_angle):
    row_index = lax.axis_index("row")
    col_index = lax.axis_index("col")
    steps, sources, orbitals, width = retarded.shape
    window = steps * lax.axis_size("row")
    panels = lesser_panel.shape[2]
    norm = 1.0 / (orbitals * math.sqrt(window))
    core = row_index % CORES
    x = (row_index // CORES) % X
    y = row_index // (CORES * X)
    where = jnp.stack([core, x, y]).astype(jnp.int32)
    way = jnp.where(core == 0, 1, -1)

    local = jnp.moveaxis(lesser_panel.reshape(orbitals, panels // 2, 2, width), 2, 0)
    local = local.reshape(2, orbitals, panels // 2 * width)
    times = jnp.stack([row_index * steps, col_index * sources]).astype(jnp.int32)
    energy = energy_call(retarded, mirrored, slot_table(row_index), times)

    def cols_of(rels):
        return ((col_index + way * jnp.array(rels, jnp.int32)) % Z).astype(jnp.int32)

    line0, line1 = near_line(local)
    blocks0 = far_blocks(line0)
    blocks1 = far_blocks(line1)
    panels0 = blocks0 + [send(block, CORE_SWAP) for block in blocks0]
    parts0 = column_sum(norm, cols_of, energy, panels0)
    panels1 = blocks1 + [send(block, CORE_SWAP) for block in blocks1]
    parts1 = column_sum(norm, cols_of, energy, panels1)

    rotate_re = retention * jnp.cos(phase_angle)[None, :]
    rotate_im = retention * jnp.sin(phase_angle)[None, :]
    lane = jnp.arange(width, dtype=jnp.int32)
    sign = jnp.where(lane < orbitals, -1.0, 1.0).astype(jnp.float32)
    fre = jnp.broadcast_to(rotate_re[:, :, None], (steps, orbitals, width))
    fim = rotate_im[:, :, None] * sign
    start = jnp.swapaxes(initial, 0, 1)

    message = jax.ShapeDtypeStruct((3, orbitals, width), jnp.float32)
    total = jax.ShapeDtypeStruct((steps, orbitals, width), jnp.float32)
    end = jax.ShapeDtypeStruct((orbitals, width), jnp.float32)
    sum0, end0 = small_call(end_kernel, (total, end), None, fre, fim, *parts0)
    sum1, end1 = small_call(end_kernel, (total, end), None, fre, fim, *parts1)
    ends = small_call(message_kernel, message, None, fre, fim, end0, end1)
    other = send(ends, CORE_SWAP)
    chip = small_call(chip_kernel, message, where, ends, other)
    row_perm = lambda by: perm_of(lambda y, x, core, z: (y, x + by, core, z))
    column_perm = lambda by: perm_of(lambda y, x, core, z: (y + by, x, core, z))
    behind = [send(chip, row_perm(back)) for back in (1, 2, 3)]

    def across(*refs):
        line_kernel(1, *refs)

    before_x, line = small_call(across, (message, message), where, chip, *behind)
    behind = [send(line, column_perm(back)) for back in (1, 2, 3)]
    before_y = small_call(column_kernel, message, where, line, *behind)
    out = small_call(
        last_kernel,
        jax.ShapeDtypeStruct((steps, 2, orbitals, width), jnp.float32),
        where,
        fre,
        fim,
        sum0,
        sum1,
        start,
        before_y,
        before_x,
        other,
    )
    return jnp.swapaxes(out, 1, 2)


def solution(mesh):
    return jax.shard_map(
        per_device,
        mesh=mesh,
        in_specs=(
            P("row", "col", None, None),
            P("col", "row", None, None),
            P(("col", "row"), None, None, None),
            P(None, "col", None),
            P("row", None),
            P(),
        ),
        out_specs=P("row", None, "col", None),
        check_vma=False,
    )
```

```python
import math

import jax
import jax.numpy as jnp
from jax import lax
from jax.experimental import pallas as pl
from jax.experimental.pallas import tpu as pltpu
from jax.sharding import PartitionSpec as P


Y, X, CORES, Z = 4, 4, 2, 8
OFFSETS = (0, -1, 1, 2)
BOTH = ("row", "col")


def joint(y, x, core, z):
    return (((y % Y) * X + (x % X)) * CORES + core) * Z + z % Z


def perm_of(target):
    pairs = []
    for y in range(Y):
        for x in range(X):
            for core in range(CORES):
                for z in range(Z):
                    pairs.append((joint(y, x, core, z), joint(*target(y, x, core, z))))
    return pairs


def plane_perm(by, first):
    return perm_of(
        lambda y, x, core, z: (y, x + by, core, z)
        if (core == 0) == first
        else (y + by, x, core, z)
    )


def depth_perm(by):
    return perm_of(lambda y, x, core, z: (y, x, core, z + (by if core == 0 else -by)))


CORE_SWAP = perm_of(lambda y, x, core, z: (y, x, 1 - core, z))


def send(array, perm):
    return lax.ppermute(array, BOTH, perm)


def energy_kernel(slots, times, ret_ref, mir_ref, out_ref):
    orbitals = ret_ref.shape[2]
    slot_count = ret_ref.shape[1]
    now = times[0] + pl.program_id(0)
    first_source = times[1]
    low = lax.broadcasted_iota(jnp.int32, (orbitals, 2 * orbitals), 1) < orbitals
    low_row = lax.broadcasted_iota(jnp.int32, (1, 2 * orbitals), 1) < orbitals

    def pair(n, carry):
        s0 = slots[2 * n]
        s1 = slots[2 * n + 1]
        a0 = ret_ref[0, s0].astype(jnp.float32)
        a1 = ret_ref[0, s1].astype(jnp.float32)
        b = jnp.concatenate([mir_ref[s0, 0], mir_ref[s1, 0]], axis=0).astype(jnp.float32)
        keep0 = jnp.where(first_source + s0 <= now, 1.0, 0.0)
        keep1 = jnp.where(first_source + s1 <= now, 1.0, 0.0)
        keep = jnp.where(low_row, keep0, keep1)
        bt = b.T
        b_re = bt[:orbitals] * keep
        b_im = bt[orbitals:] * keep
        re = jnp.where(low, a0, pltpu.roll(a1, orbitals, 1))
        im = jnp.where(low, pltpu.roll(a0, orbitals, 1), a1)
        sq_re = re * re - im * im
        sq_im = 2.0 * re * im
        cols = pl.ds(pl.multiple_of(n * 2 * orbitals, 2 * orbitals), 2 * orbitals)
        out_ref[0, 0, :, cols] = (sq_re * b_re - sq_im * b_im).astype(jnp.bfloat16)
        out_ref[0, 1, :, cols] = (sq_re * b_im + sq_im * b_re).astype(jnp.bfloat16)
        return carry

    lax.fori_loop(0, slot_count // 2, pair, 0, unroll=4)


def energy_call(retarded, mirrored, slots, times):
    steps, sources, orbitals, width = retarded.shape
    return pl.pallas_call(
        energy_kernel,
        out_shape=jax.ShapeDtypeStruct((steps, 2, orbitals, sources * orbitals), jnp.bfloat16),
        grid_spec=pltpu.PrefetchScalarGridSpec(
            num_scalar_prefetch=2,
            grid=(steps,),
            in_specs=[
                pl.BlockSpec((1, sources, orbitals, width), lambda t, *_: (t, 0, 0, 0)),
                pl.BlockSpec((sources, 1, orbitals, width), lambda t, *_: (0, t, 0, 0)),
            ],
            out_specs=pl.BlockSpec(
                (1, 2, orbitals, sources * orbitals), lambda t, *_: (t, 0, 0, 0)
            ),
        ),
        compiler_params=pltpu.CompilerParams(vmem_limit_bytes=14 << 20),
        cost_estimate=pl.CostEstimate(
            flops=20 * steps * sources * orbitals * width,
            bytes_accessed=6 * steps * sources * orbitals * width,
            transcendentals=0,
        ),
    )(
        slots,
        times,
        pltpu.with_memory_space_constraint(retarded, pltpu.HBM),
        pltpu.with_memory_space_constraint(mirrored, pltpu.HBM),
    )


def product_call(norm, cols, energy, panels, kinds):
    steps, _, orbitals, depth = energy.shape
    width = 2 * orbitals
    shape = [jax.ShapeDtypeStruct((count, steps, orbitals, width), kind) for count, kind in kinds]
    places = [(n, at) for n, (count, _) in enumerate(kinds) for at in range(count)]
    pieces, tiles = len(panels), len(places)

    def body(cols_ref, energy_ref, *refs):
        panel_refs, out_refs = refs[: tiles * pieces], refs[tiles * pieces :]
        left = energy_ref[...].reshape(steps * 2 * orbitals, depth)
        right = jnp.concatenate(
            [
                jnp.concatenate(
                    [ref[...] for ref in panel_refs[tile * pieces : (tile + 1) * pieces]], axis=0
                )
                for tile in range(tiles)
            ],
            axis=1,
        )
        both = jnp.dot(left, right, preferred_element_type=jnp.float32)
        both = both.reshape(steps, 2, orbitals, tiles * width)
        lane = lax.broadcasted_iota(jnp.int32, (steps, orbitals, width), 2)
        sign = jnp.where(lane < orbitals, -norm, norm)
        for tile, (result, at) in enumerate(places):
            part_re = both[:, 0, :, tile * width : (tile + 1) * width]
            part_im = both[:, 1, :, tile * width : (tile + 1) * width]
            value = part_re * norm + sign * pltpu.roll(part_im, orbitals, 2)
            out_refs[result][at] = value.astype(kinds[result][1])

    def panel_spec(panel, tile):
        return pl.BlockSpec((panel.shape[0], width), lambda n, cols: (0, cols[tile]))

    return pl.pallas_call(
        body,
        out_shape=shape,
        grid_spec=pltpu.PrefetchScalarGridSpec(
            num_scalar_prefetch=1,
            grid=(1,),
            in_specs=[pl.BlockSpec(memory_space=pltpu.VMEM)]
            + [panel_spec(panel, tile) for tile in range(tiles) for panel in panels],
            out_specs=[pl.BlockSpec(s.shape, lambda n, cols: (0, 0, 0, 0)) for s in shape],
        ),
        compiler_params=pltpu.CompilerParams(vmem_limit_bytes=32 << 20),
        cost_estimate=pl.CostEstimate(
            flops=2 * tiles * steps * 2 * orbitals * depth * width,
            bytes_accessed=2 * depth * (steps * 2 * orbitals + tiles * width),
            transcendentals=0,
        ),
    )(cols, energy, *(panels * tiles))


def turned(factor_re, factor_im, value):
    return factor_re * value + factor_im * pltpu.roll(value, value.shape[-1] // 2, value.ndim - 1)


def end_of(fre_ref, fim_ref, parts, sum_ref):
    own_ref, ahead_ref, back_ref, from5_ref, from3_ref = parts
    steps, orbitals, width = sum_ref.shape
    state = jnp.zeros((orbitals, width), jnp.float32)
    for t in range(steps):
        value = own_ref[0, t]
        for arrived in (ahead_ref[2, t], back_ref[1, t], from5_ref[t], from3_ref[t]):
            value = value + arrived.astype(jnp.float32)
        sum_ref[t] = value
        state = turned(fre_ref[t], fim_ref[t], state + value)
    return state


def even_kernel(fre_ref, fim_ref, *refs):
    parts, (sum_ref, end_ref) = refs[:-2], refs[-2:]
    end_ref[...] = end_of(fre_ref, fim_ref, parts, sum_ref)


def odd_kernel(fre_ref, fim_ref, even_ref, *refs):
    parts, (sum_ref, msg_ref) = refs[:-2], refs[-2:]
    steps, orbitals, width = fre_ref.shape
    lane = lax.broadcasted_iota(jnp.int32, (orbitals, width), 1)
    block = jnp.where(lane < width // 2, 1.0, 0.0).astype(jnp.float32)
    for t in range(steps):
        block = turned(fre_ref[t], fim_ref[t], block)
    msg_ref[0] = even_ref[...]
    msg_ref[1] = end_of(fre_ref, fim_ref, parts, sum_ref)
    msg_ref[2] = block


def apply(later, earlier):
    width = later.shape[-1]
    lane = lax.broadcasted_iota(jnp.int32, later.shape[1:], 1)
    low = lane < width // 2
    factor = later[2]
    swapped = pltpu.roll(factor, width // 2, 1)
    fre = jnp.where(low, factor, swapped)
    fim = jnp.where(low, -swapped, factor)
    planes = [
        turned(fre, fim, earlier[0]) + later[0],
        turned(fre, fim, earlier[1]) + later[1],
        turned(fre, fim, earlier[2]),
    ]
    return planes


def chosen(keep, planes, other):
    return [jnp.where(keep, a, b) for a, b in zip(planes, other)]


def unit(shape):
    lane = lax.broadcasted_iota(jnp.int32, shape, 1)
    return [
        jnp.zeros(shape, jnp.float32),
        jnp.zeros(shape, jnp.float32),
        jnp.where(lane < shape[-1] // 2, 1.0, 0.0).astype(jnp.float32),
    ]


def read(ref):
    return [ref[0], ref[1], ref[2]]


class Planes:
    def __init__(self, planes):
        self.planes = planes
        self.shape = (3,) + planes[0].shape

    def __getitem__(self, index):
        return self.planes[index]


def after(later, earlier):
    return apply(Planes(later), Planes(earlier))


def chip_kernel(where_ref, own_ref, other_ref, out_ref):
    odd = where_ref[0] == 1
    own, other = read(own_ref), read(other_ref)
    later = chosen(odd, own, other)
    earlier = chosen(odd, other, own)
    for n, plane in enumerate(after(later, earlier)):
        out_ref[n] = plane


def before_of(at, behind, one):
    before = one
    for back in (3, 2, 1):
        here = chosen(at >= back, behind[back - 1], one)
        before = after(here, before)
    return before


def line_kernel(where_ref, own_ref, d1_ref, d2_ref, d3_ref, before_ref, total_ref):
    at = where_ref[1]
    one = unit(own_ref.shape[1:])
    behind = [read(d1_ref), read(d2_ref), read(d3_ref)]
    before = before_of(at, behind, one)
    for n, plane in enumerate(before):
        before_ref[n] = plane
    total = after(read(own_ref), before)
    for back in (3, 2, 1):
        here = chosen(at < back, behind[back - 1], one)
        total = after(here, total)
    for n, plane in enumerate(total):
        total_ref[n] = plane


def last_kernel(
    where_ref,
    fre_ref,
    fim_ref,
    sum0_ref,
    sum1_ref,
    init_ref,
    d1_ref,
    d2_ref,
    d3_ref,
    x_ref,
    core_ref,
    out_ref,
):
    steps = fre_ref.shape[0]
    one = unit(init_ref.shape[1:])
    column = before_of(where_ref[2], [read(d1_ref), read(d2_ref), read(d3_ref)], one)
    start = after(column, [init_ref[0], init_ref[1], one[2]])
    start = after(read(x_ref), start)
    start = after(chosen(where_ref[0] == 1, read(core_ref), one), start)
    for half, sum_ref in enumerate((sum0_ref, sum1_ref)):
        state = start[half]
        for t in range(steps):
            state = turned(fre_ref[t], fim_ref[t], state + sum_ref[t])
            out_ref[t, :, half, :] = state


def small_call(kernel, out_shape, scalars, *arrays):
    specs = [pl.BlockSpec(memory_space=pltpu.SMEM)] if scalars is not None else []
    specs += [pl.BlockSpec(memory_space=pltpu.VMEM)] * len(arrays)
    out_specs = jax.tree.map(lambda _: pl.BlockSpec(memory_space=pltpu.VMEM), out_shape)
    args = ([scalars] if scalars is not None else []) + list(arrays)
    return pl.pallas_call(
        kernel,
        out_shape=out_shape,
        in_specs=specs,
        out_specs=out_specs,
        compiler_params=pltpu.CompilerParams(vmem_limit_bytes=8 << 20),
        cost_estimate=pl.CostEstimate(flops=1000000, bytes_accessed=1 << 20, transcendentals=0),
    )(*args)


def near_line(local):
    moved = [local] + [send(local, plane_perm(-off, True)) for off in OFFSETS[1:]]
    return [jnp.concatenate([m[chunk] for m in moved], axis=0) for chunk in range(2)]


def far_blocks(line):
    blocks = [line]
    for off in OFFSETS[1:]:
        blocks.append(send(line, plane_perm(-off, False)))
    return blocks


def add_rounded(*parts):
    total = parts[0]
    for part in parts[1:]:
        total = total + part.astype(jnp.float32)
    return total.astype(jnp.bfloat16)


def column_sum(norm, cols_of, energy, panels, split):
    near = ((3, jnp.bfloat16), (2, jnp.bfloat16), (1, jnp.float32))
    far = ((2, jnp.float32),)
    order = (4, 6, 1, 2, 7, 0, 3, 5)
    if split:
        ahead, back, own = product_call(norm, cols_of(order[:6]), energy, panels, near)
    else:
        ahead, back, own, rest = product_call(norm, cols_of(order), energy, panels, near + far)
    ahead = send(ahead, depth_perm(1))
    back = send(back, depth_perm(-1))
    if split:
        (rest,) = product_call(norm, cols_of(order[6:]), energy, panels, far)
    from5 = send(add_rounded(rest[1], ahead[1]), depth_perm(-3))
    from3 = send(add_rounded(rest[0], ahead[0], back[0]), depth_perm(3))
    return [own, ahead, back, from5, from3]


def slot_table(row_index):
    core = row_index % CORES
    x = (row_index // CORES) % X
    y = row_index // (CORES * X)
    offs = jnp.array(OFFSETS, jnp.int32)
    outer = jnp.repeat(offs, len(OFFSETS))
    inner = jnp.tile(offs, len(OFFSETS))

    def of(which):
        dy = jnp.where(which == 0, outer, inner)
        dx = jnp.where(which == 0, inner, outer)
        return (((y + dy) % Y) * X + (x + dx) % X) * CORES + which

    return jnp.concatenate([of(core), of(1 - core)]).astype(jnp.int32)


def per_device(retarded, mirrored, lesser_panel, initial, retention, phase_angle):
    row_index = lax.axis_index("row")
    col_index = lax.axis_index("col")
    steps, sources, orbitals, width = retarded.shape
    window = steps * lax.axis_size("row")
    panels = lesser_panel.shape[2]
    norm = 1.0 / (orbitals * math.sqrt(window))
    core = row_index % CORES
    x = (row_index // CORES) % X
    y = row_index // (CORES * X)
    where = jnp.stack([core, x, y]).astype(jnp.int32)
    way = jnp.where(core == 0, 1, -1)

    local = jnp.moveaxis(lesser_panel.reshape(orbitals, panels // 2, 2, width), 2, 0)
    local = local.reshape(2, orbitals, panels // 2 * width)
    times = jnp.stack([row_index * steps, col_index * sources]).astype(jnp.int32)
    energy = energy_call(retarded, mirrored, slot_table(row_index), times)

    def cols_of(rels):
        return ((col_index + way * jnp.array(rels, jnp.int32)) % Z).astype(jnp.int32)

    line0, line1 = near_line(local)
    blocks0 = far_blocks(line0)
    blocks1 = far_blocks(line1)
    panels0 = blocks0 + [send(block, CORE_SWAP) for block in blocks0]
    parts0 = column_sum(norm, cols_of, energy, panels0, False)
    panels1 = list(blocks1)
    for block in blocks1:
        panels1.append(send(block, CORE_SWAP))
    parts1 = column_sum(norm, cols_of, energy, panels1, True)

    rotate_re = retention * jnp.cos(phase_angle)[None, :]
    rotate_im = retention * jnp.sin(phase_angle)[None, :]
    lane = jnp.arange(width, dtype=jnp.int32)
    sign = jnp.where(lane < orbitals, -1.0, 1.0).astype(jnp.float32)
    fre = jnp.broadcast_to(rotate_re[:, :, None], (steps, orbitals, width))
    fim = rotate_im[:, :, None] * sign
    start = jnp.swapaxes(initial, 0, 1)

    message = jax.ShapeDtypeStruct((3, orbitals, width), jnp.float32)
    total = jax.ShapeDtypeStruct((steps, orbitals, width), jnp.float32)
    end = jax.ShapeDtypeStruct((orbitals, width), jnp.float32)
    sum0, end0 = small_call(even_kernel, (total, end), None, fre, fim, *parts0)
    sum1, ends = small_call(odd_kernel, (total, message), None, fre, fim, end0, *parts1)
    other = send(ends, CORE_SWAP)
    chip = small_call(chip_kernel, message, where, ends, other)
    row_perm = lambda by: perm_of(lambda y, x, core, z: (y, x + by, core, z))
    column_perm = lambda by: perm_of(lambda y, x, core, z: (y + by, x, core, z))
    behind = [send(chip, row_perm(back)) for back in (1, 2, 3)]

    before_x, line = small_call(line_kernel, (message, message), where, chip, *behind)
    behind = [send(line, column_perm(back)) for back in (1, 2, 3)]
    return small_call(
        last_kernel,
        jax.ShapeDtypeStruct((steps, orbitals, 2, width), jnp.float32),
        where,
        fre,
        fim,
        sum0,
        sum1,
        start,
        *behind,
        before_x,
        other,
    )


def solution(mesh):
    return jax.shard_map(
        per_device,
        mesh=mesh,
        in_specs=(
            P("row", "col", None, None),
            P("col", "row", None, None),
            P(("col", "row"), None, None, None),
            P(None, "col", None),
            P("row", None),
            P(),
        ),
        out_specs=P("row", None, "col", None),
        check_vma=False,
    )
```

```python
import math

import jax
import jax.numpy as jnp
from jax import lax
from jax.experimental import pallas as pl
from jax.experimental.pallas import tpu as pltpu
from jax.sharding import PartitionSpec as P


Y, X, CORES, Z = 4, 4, 2, 8
OFFSETS = (0, -1, 1, 2)
BOTH = ("row", "col")


def joint(y, x, core, z):
    return (((y % Y) * X + (x % X)) * CORES + core) * Z + z % Z


def perm_of(target):
    pairs = []
    for y in range(Y):
        for x in range(X):
            for core in range(CORES):
                for z in range(Z):
                    pairs.append((joint(y, x, core, z), joint(*target(y, x, core, z))))
    return pairs


def plane_perm(by, first):
    return perm_of(
        lambda y, x, core, z: (y, x + by, core, z)
        if (core == 0) == first
        else (y + by, x, core, z)
    )


def depth_perm(by):
    return perm_of(lambda y, x, core, z: (y, x, core, z + (by if core == 0 else -by)))


CORE_SWAP = perm_of(lambda y, x, core, z: (y, x, 1 - core, z))


def send(array, perm):
    return lax.ppermute(array, BOTH, perm)


def energy_kernel(slots, times, ret_ref, mir_ref, out_ref):
    orbitals = ret_ref.shape[2]
    slot_count = ret_ref.shape[1]
    now = times[0] + pl.program_id(0)
    first_source = times[1]
    low = lax.broadcasted_iota(jnp.int32, (orbitals, 2 * orbitals), 1) < orbitals
    low_row = lax.broadcasted_iota(jnp.int32, (1, 2 * orbitals), 1) < orbitals

    def pair(n, carry):
        s0 = slots[2 * n]
        s1 = slots[2 * n + 1]
        a0 = ret_ref[0, s0].astype(jnp.float32)
        a1 = ret_ref[0, s1].astype(jnp.float32)
        b = jnp.concatenate([mir_ref[s0, 0], mir_ref[s1, 0]], axis=0).astype(jnp.float32)
        keep0 = jnp.where(first_source + s0 <= now, 1.0, 0.0)
        keep1 = jnp.where(first_source + s1 <= now, 1.0, 0.0)
        keep = jnp.where(low_row, keep0, keep1)
        bt = b.T
        b_re = bt[:orbitals] * keep
        b_im = bt[orbitals:] * keep
        re = jnp.where(low, a0, pltpu.roll(a1, orbitals, 1))
        im = jnp.where(low, pltpu.roll(a0, orbitals, 1), a1)
        sq_re = re * re - im * im
        sq_im = 2.0 * re * im
        cols = pl.ds(pl.multiple_of(n * 2 * orbitals, 2 * orbitals), 2 * orbitals)
        out_ref[0, 0, :, cols] = (sq_re * b_re - sq_im * b_im).astype(jnp.bfloat16)
        out_ref[0, 1, :, cols] = (sq_re * b_im + sq_im * b_re).astype(jnp.bfloat16)
        return carry

    lax.fori_loop(0, slot_count // 2, pair, 0, unroll=4)


def energy_call(retarded, mirrored, slots, times):
    steps, sources, orbitals, width = retarded.shape
    return pl.pallas_call(
        energy_kernel,
        out_shape=jax.ShapeDtypeStruct((steps, 2, orbitals, sources * orbitals), jnp.bfloat16),
        grid_spec=pltpu.PrefetchScalarGridSpec(
            num_scalar_prefetch=2,
            grid=(steps,),
            in_specs=[
                pl.BlockSpec((1, sources, orbitals, width), lambda t, *_: (t, 0, 0, 0)),
                pl.BlockSpec((sources, 1, orbitals, width), lambda t, *_: (0, t, 0, 0)),
            ],
            out_specs=pl.BlockSpec(
                (1, 2, orbitals, sources * orbitals), lambda t, *_: (t, 0, 0, 0)
            ),
        ),
        compiler_params=pltpu.CompilerParams(vmem_limit_bytes=14 << 20),
        cost_estimate=pl.CostEstimate(
            flops=20 * steps * sources * orbitals * width,
            bytes_accessed=6 * steps * sources * orbitals * width,
            transcendentals=0,
        ),
    )(
        slots,
        times,
        pltpu.with_memory_space_constraint(retarded, pltpu.HBM),
        pltpu.with_memory_space_constraint(mirrored, pltpu.HBM),
    )


def turned(factor_re, factor_im, value):
    return factor_re * value + factor_im * pltpu.roll(value, value.shape[-1] // 2, value.ndim - 1)


def product_call(norm, cols, energy, factors, panels, kinds, even_ends=None):
    steps, _, orbitals, depth = energy.shape
    width = 2 * orbitals
    shape = [jax.ShapeDtypeStruct((count, steps, orbitals, width), kind) for count, kind in kinds]
    places = [(n, at) for n, (count, _) in enumerate(kinds) for at in range(count)]
    pieces, tiles = len(panels), len(places)
    first = len(shape)
    if even_ends is None:
        shape.append(jax.ShapeDtypeStruct((tiles, orbitals, width), jnp.float32))
        extra = []
    else:
        shape += [
            jax.ShapeDtypeStruct((count, 2, orbitals, width), kind)
            for count, kind in ((3, jnp.bfloat16), (2, jnp.bfloat16), (3, jnp.float32))
        ]
        extra = [even_ends]
    packed = [(0, 0), (0, 1), (0, 2), (1, 0), (1, 1), (2, 0), (2, 1), (2, 2)]

    def body(cols_ref, energy_ref, fre_ref, fim_ref, *refs):
        even_refs, refs = refs[: len(extra)], refs[len(extra) :]
        panel_refs, out_refs = refs[: tiles * pieces], refs[tiles * pieces :]
        left = energy_ref[...].reshape(steps * 2 * orbitals, depth)
        right = jnp.concatenate(
            [
                jnp.concatenate(
                    [ref[...] for ref in panel_refs[tile * pieces : (tile + 1) * pieces]], axis=0
                )
                for tile in range(tiles)
            ],
            axis=1,
        )
        both = jnp.dot(left, right, preferred_element_type=jnp.float32)
        both = both.reshape(steps, 2, orbitals, tiles * width)
        lane = lax.broadcasted_iota(jnp.int32, (steps, orbitals, width), 2)
        sign = jnp.where(lane < orbitals, -norm, norm)
        for tile, (result, at) in enumerate(places):
            part_re = both[:, 0, :, tile * width : (tile + 1) * width]
            part_im = both[:, 1, :, tile * width : (tile + 1) * width]
            value = part_re * norm + sign * pltpu.roll(part_im, orbitals, 2)
            out_refs[result][at] = value.astype(kinds[result][1])
            end = jnp.zeros((orbitals, width), jnp.float32)
            for t in range(steps):
                end = turned(fre_ref[t], fim_ref[t], end + value[t])
            if not extra:
                out_refs[first][tile] = end
            else:
                group, place = packed[tile]
                target = out_refs[first + group]
                target[place, 0] = even_refs[0][tile].astype(target.dtype)
                target[place, 1] = end.astype(target.dtype)

    def panel_spec(panel, tile):
        return pl.BlockSpec((panel.shape[0], width), lambda n, cols: (0, cols[tile]))

    return pl.pallas_call(
        body,
        out_shape=shape,
        grid_spec=pltpu.PrefetchScalarGridSpec(
            num_scalar_prefetch=1,
            grid=(1,),
            in_specs=[pl.BlockSpec(memory_space=pltpu.VMEM)] * (3 + len(extra))
            + [panel_spec(panel, tile) for tile in range(tiles) for panel in panels],
            out_specs=[pl.BlockSpec(memory_space=pltpu.VMEM)] * len(shape),
        ),
        compiler_params=pltpu.CompilerParams(vmem_limit_bytes=34 << 20),
        cost_estimate=pl.CostEstimate(
            flops=2 * tiles * steps * 2 * orbitals * depth * width,
            bytes_accessed=2 * depth * (steps * 2 * orbitals + tiles * width),
            transcendentals=0,
        ),
    )(cols, energy, *factors, *extra, *(panels * tiles))


def sum_kernel(own_ref, ahead_ref, back_ref, from5_ref, from3_ref, sum_ref):
    value = own_ref[0]
    for arrived in (ahead_ref[2], back_ref[1], from5_ref[...], from3_ref[...]):
        value = value + arrived.astype(jnp.float32)
    sum_ref[...] = value


def message_kernel(fre_ref, fim_ref, own_ref, ahead_ref, back_ref, from5_ref, from3_ref, msg_ref):
    steps, orbitals, width = fre_ref.shape
    lane = lax.broadcasted_iota(jnp.int32, (orbitals, width), 1)
    block = jnp.where(lane < width // 2, 1.0, 0.0).astype(jnp.float32)
    for t in range(steps):
        block = turned(fre_ref[t], fim_ref[t], block)
    for half in range(2):
        value = own_ref[0, half]
        for arrived in (ahead_ref[2, half], back_ref[1, half], from5_ref[half], from3_ref[half]):
            value = value + arrived.astype(jnp.float32)
        msg_ref[half] = value
    msg_ref[2] = block


def apply(later, earlier):
    width = later.shape[-1]
    lane = lax.broadcasted_iota(jnp.int32, later.shape[1:], 1)
    low = lane < width // 2
    factor = later[2]
    swapped = pltpu.roll(factor, width // 2, 1)
    fre = jnp.where(low, factor, swapped)
    fim = jnp.where(low, -swapped, factor)
    planes = [
        turned(fre, fim, earlier[0]) + later[0],
        turned(fre, fim, earlier[1]) + later[1],
        turned(fre, fim, earlier[2]),
    ]
    return planes


def chosen(keep, planes, other):
    return [jnp.where(keep, a, b) for a, b in zip(planes, other)]


def unit(shape):
    lane = lax.broadcasted_iota(jnp.int32, shape, 1)
    return [
        jnp.zeros(shape, jnp.float32),
        jnp.zeros(shape, jnp.float32),
        jnp.where(lane < shape[-1] // 2, 1.0, 0.0).astype(jnp.float32),
    ]


def read(ref):
    return [ref[0], ref[1], ref[2]]


class Planes:
    def __init__(self, planes):
        self.planes = planes
        self.shape = (3,) + planes[0].shape

    def __getitem__(self, index):
        return self.planes[index]


def after(later, earlier):
    return apply(Planes(later), Planes(earlier))


def chip_kernel(where_ref, own_ref, other_ref, out_ref):
    odd = where_ref[0] == 1
    own, other = read(own_ref), read(other_ref)
    later = chosen(odd, own, other)
    earlier = chosen(odd, other, own)
    for n, plane in enumerate(after(later, earlier)):
        out_ref[n] = plane


def before_of(at, behind, one):
    before = one
    for back in (3, 2, 1):
        here = chosen(at >= back, behind[back - 1], one)
        before = after(here, before)
    return before


def line_kernel(where_ref, own_ref, d1_ref, d2_ref, d3_ref, before_ref, total_ref):
    at = where_ref[1]
    one = unit(own_ref.shape[1:])
    behind = [read(d1_ref), read(d2_ref), read(d3_ref)]
    before = before_of(at, behind, one)
    for n, plane in enumerate(before):
        before_ref[n] = plane
    total = after(read(own_ref), before)
    for back in (3, 2, 1):
        here = chosen(at < back, behind[back - 1], one)
        total = after(here, total)
    for n, plane in enumerate(total):
        total_ref[n] = plane


def enter_kernel(where_ref, init_ref, d1_ref, d2_ref, d3_ref, x_ref, core_ref, out_ref):
    one = unit(init_ref.shape[1:])
    column = before_of(where_ref[2], [read(d1_ref), read(d2_ref), read(d3_ref)], one)
    start = after(column, [init_ref[0], init_ref[1], one[2]])
    start = after(read(x_ref), start)
    start = after(chosen(where_ref[0] == 1, read(core_ref), one), start)
    for half in range(2):
        out_ref[half] = start[half]


def last_kernel(
    fre_ref, fim_ref, enter_ref, even_ref, own_ref, ahead_ref, back_ref, from5_ref, from3_ref, out_ref
):
    steps = fre_ref.shape[0]
    even, odd = enter_ref[0], enter_ref[1]
    for t in range(steps):
        value = own_ref[0, t]
        for arrived in (ahead_ref[2, t], back_ref[1, t], from5_ref[t], from3_ref[t]):
            value = value + arrived.astype(jnp.float32)
        even = turned(fre_ref[t], fim_ref[t], even + even_ref[t])
        odd = turned(fre_ref[t], fim_ref[t], odd + value)
        out_ref[t, :, 0, :] = even
        out_ref[t, :, 1, :] = odd


def small_call(kernel, out_shape, scalars, *arrays):
    specs = [pl.BlockSpec(memory_space=pltpu.SMEM)] if scalars is not None else []
    specs += [pl.BlockSpec(memory_space=pltpu.VMEM)] * len(arrays)
    out_specs = jax.tree.map(lambda _: pl.BlockSpec(memory_space=pltpu.VMEM), out_shape)
    args = ([scalars] if scalars is not None else []) + list(arrays)
    return pl.pallas_call(
        kernel,
        out_shape=out_shape,
        in_specs=specs,
        out_specs=out_specs,
        compiler_params=pltpu.CompilerParams(vmem_limit_bytes=8 << 20),
        cost_estimate=pl.CostEstimate(flops=1000000, bytes_accessed=1 << 20, transcendentals=0),
    )(*args)


def near_line(local):
    moved = [local] + [send(local, plane_perm(-off, True)) for off in OFFSETS[1:]]
    return [jnp.concatenate([m[chunk] for m in moved], axis=0) for chunk in range(2)]


def far_blocks(line):
    blocks = [line]
    for off in OFFSETS[1:]:
        blocks.append(send(line, plane_perm(-off, False)))
    return blocks


def add_rounded(*parts):
    total = parts[0]
    for part in parts[1:]:
        total = total + part.astype(jnp.float32)
    return total.astype(jnp.bfloat16)


SHARES = (4, 6, 1, 2, 7, 0, 3, 5)


def column_product(norm, cols_of, energy, factors, panels, even_ends=None):
    kinds = ((3, jnp.bfloat16), (2, jnp.bfloat16), (1, jnp.float32), (2, jnp.float32))
    return product_call(norm, cols_of(SHARES), energy, factors, panels, kinds, even_ends)


def column_sum(ahead, back, rest):
    ahead = send(ahead, depth_perm(1))
    back = send(back, depth_perm(-1))
    from5 = send(add_rounded(rest[1], ahead[1]), depth_perm(-3))
    from3 = send(add_rounded(rest[0], ahead[0], back[0]), depth_perm(3))
    return [ahead, back, from5, from3]


def slot_table(row_index):
    core = row_index % CORES
    x = (row_index // CORES) % X
    y = row_index // (CORES * X)
    offs = jnp.array(OFFSETS, jnp.int32)
    outer = jnp.repeat(offs, len(OFFSETS))
    inner = jnp.tile(offs, len(OFFSETS))

    def of(which):
        dy = jnp.where(which == 0, outer, inner)
        dx = jnp.where(which == 0, inner, outer)
        return (((y + dy) % Y) * X + (x + dx) % X) * CORES + which

    return jnp.concatenate([of(core), of(1 - core)]).astype(jnp.int32)


def per_device(retarded, mirrored, lesser_panel, initial, retention, phase_angle):
    row_index = lax.axis_index("row")
    col_index = lax.axis_index("col")
    steps, sources, orbitals, width = retarded.shape
    window = steps * lax.axis_size("row")
    panels = lesser_panel.shape[2]
    norm = 1.0 / (orbitals * math.sqrt(window))
    core = row_index % CORES
    x = (row_index // CORES) % X
    y = row_index // (CORES * X)
    where = jnp.stack([core, x, y]).astype(jnp.int32)
    way = jnp.where(core == 0, 1, -1)

    local = jnp.moveaxis(lesser_panel.reshape(orbitals, panels // 2, 2, width), 2, 0)
    local = local.reshape(2, orbitals, panels // 2 * width)
    times = jnp.stack([row_index * steps, col_index * sources]).astype(jnp.int32)
    energy = energy_call(retarded, mirrored, slot_table(row_index), times)

    def cols_of(rels):
        return ((col_index + way * jnp.array(rels, jnp.int32)) % Z).astype(jnp.int32)

    rotate_re = retention * jnp.cos(phase_angle)[None, :]
    rotate_im = retention * jnp.sin(phase_angle)[None, :]
    lane = jnp.arange(width, dtype=jnp.int32)
    sign = jnp.where(lane < orbitals, -1.0, 1.0).astype(jnp.float32)
    fre = jnp.broadcast_to(rotate_re[:, :, None], (steps, orbitals, width))
    fim = rotate_im[:, :, None] * sign
    start = jnp.swapaxes(initial, 0, 1)


    line0, line1 = near_line(local)
    blocks0 = far_blocks(line0)
    blocks1 = far_blocks(line1)
    panels0 = blocks0 + [send(block, CORE_SWAP) for block in blocks0]
    factors = (fre, fim)
    *terms0, own0, rest0, ends0 = column_product(norm, cols_of, energy, factors, panels0)
    parts0 = column_sum(*terms0, rest0)
    panels1 = list(blocks1)
    for block in blocks1:
        panels1.append(send(block, CORE_SWAP))
    *terms1, own1, rest1, ends_ahead, ends_back, ends_rest = column_product(
        norm, cols_of, energy, factors, panels1, ends0
    )
    end_parts = column_sum(ends_ahead, ends_back, ends_rest[1:])
    parts1 = column_sum(*terms1, rest1)

    message = jax.ShapeDtypeStruct((3, orbitals, width), jnp.float32)
    total = jax.ShapeDtypeStruct((steps, orbitals, width), jnp.float32)
    sum0 = small_call(sum_kernel, total, None, own0, *parts0)
    ends = small_call(message_kernel, message, None, fre, fim, ends_rest, *end_parts)
    other = send(ends, CORE_SWAP)
    chip = small_call(chip_kernel, message, where, ends, other)
    row_perm = lambda by: perm_of(lambda y, x, core, z: (y, x + by, core, z))
    column_perm = lambda by: perm_of(lambda y, x, core, z: (y + by, x, core, z))
    behind = [send(chip, row_perm(back)) for back in (1, 2, 3)]

    before_x, line = small_call(line_kernel, (message, message), where, chip, *behind)
    behind = [send(line, column_perm(back)) for back in (1, 2, 3)]
    entering = small_call(
        enter_kernel,
        jax.ShapeDtypeStruct((2, orbitals, width), jnp.float32),
        where,
        start,
        *behind,
        before_x,
        other,
    )
    return small_call(
        last_kernel,
        jax.ShapeDtypeStruct((steps, orbitals, 2, width), jnp.float32),
        None,
        fre,
        fim,
        entering,
        sum0,
        own1,
        *parts1,
    )


def solution(mesh):
    return jax.shard_map(
        per_device,
        mesh=mesh,
        in_specs=(
            P("row", "col", None, None),
            P("col", "row", None, None),
            P(("col", "row"), None, None, None),
            P(None, "col", None),
            P("row", None),
            P(),
        ),
        out_specs=P("row", None, "col", None),
        check_vma=False,
    )
```

```python
import math

import jax
import jax.numpy as jnp
from jax import lax
from jax.experimental import pallas as pl
from jax.experimental.pallas import tpu as pltpu
from jax.sharding import PartitionSpec as P


Y, X, CORES, Z = 4, 4, 2, 8
OFFSETS = (0, -1, 1, 2)
BOTH = ("row", "col")


def joint(y, x, core, z):
    return (((y % Y) * X + (x % X)) * CORES + core) * Z + z % Z


def perm_of(target):
    pairs = []
    for y in range(Y):
        for x in range(X):
            for core in range(CORES):
                for z in range(Z):
                    pairs.append((joint(y, x, core, z), joint(*target(y, x, core, z))))
    return pairs


def plane_perm(by, first):
    return perm_of(
        lambda y, x, core, z: (y, x + by, core, z)
        if (core == 0) == first
        else (y + by, x, core, z)
    )


def depth_perm(by):
    return perm_of(lambda y, x, core, z: (y, x, core, z + (by if core == 0 else -by)))


CORE_SWAP = perm_of(lambda y, x, core, z: (y, x, 1 - core, z))


def send(array, perm):
    return lax.ppermute(array, BOTH, perm)


def energy_kernel(skip, slots, times, ret_ref, mir_ref, out_ref):
    orbitals = ret_ref.shape[2]
    slot_count = ret_ref.shape[1]
    now = times[0] + skip + pl.program_id(0)
    first_source = times[1]
    low = lax.broadcasted_iota(jnp.int32, (orbitals, 2 * orbitals), 1) < orbitals
    low_row = lax.broadcasted_iota(jnp.int32, (1, 2 * orbitals), 1) < orbitals

    def pair(n, carry):
        s0 = slots[2 * n]
        s1 = slots[2 * n + 1]
        a0 = ret_ref[0, s0].astype(jnp.float32)
        a1 = ret_ref[0, s1].astype(jnp.float32)
        b = jnp.concatenate([mir_ref[s0, 0], mir_ref[s1, 0]], axis=0).astype(jnp.float32)
        keep0 = jnp.where(first_source + s0 <= now, 1.0, 0.0)
        keep1 = jnp.where(first_source + s1 <= now, 1.0, 0.0)
        keep = jnp.where(low_row, keep0, keep1)
        bt = b.T
        b_re = bt[:orbitals] * keep
        b_im = bt[orbitals:] * keep
        re = jnp.where(low, a0, pltpu.roll(a1, orbitals, 1))
        im = jnp.where(low, pltpu.roll(a0, orbitals, 1), a1)
        sq_re = re * re - im * im
        sq_im = 2.0 * re * im
        cols = pl.ds(pl.multiple_of(n * 2 * orbitals, 2 * orbitals), 2 * orbitals)
        out_ref[0, 0, :, cols] = (sq_re * b_re - sq_im * b_im).astype(jnp.bfloat16)
        out_ref[0, 1, :, cols] = (sq_re * b_im + sq_im * b_re).astype(jnp.bfloat16)
        return carry

    lax.fori_loop(0, slot_count // 2, pair, 0, unroll=4)


def energy_call(retarded, mirrored, slots, times, part, parts):
    steps, sources, orbitals, width = retarded.shape
    steps = steps // parts
    skip = part * steps
    return pl.pallas_call(
        lambda *refs: energy_kernel(skip, *refs),
        out_shape=jax.ShapeDtypeStruct((steps, 2, orbitals, sources * orbitals), jnp.bfloat16),
        grid_spec=pltpu.PrefetchScalarGridSpec(
            num_scalar_prefetch=2,
            grid=(steps,),
            in_specs=[
                pl.BlockSpec((1, sources, orbitals, width), lambda t, *_: (t + skip, 0, 0, 0)),
                pl.BlockSpec((sources, 1, orbitals, width), lambda t, *_: (0, t + skip, 0, 0)),
            ],
            out_specs=pl.BlockSpec(
                (1, 2, orbitals, sources * orbitals), lambda t, *_: (t, 0, 0, 0)
            ),
        ),
        compiler_params=pltpu.CompilerParams(vmem_limit_bytes=14 << 20),
        cost_estimate=pl.CostEstimate(
            flops=20 * steps * sources * orbitals * width,
            bytes_accessed=6 * steps * sources * orbitals * width,
            transcendentals=0,
        ),
    )(
        slots,
        times,
        pltpu.with_memory_space_constraint(retarded, pltpu.HBM),
        pltpu.with_memory_space_constraint(mirrored, pltpu.HBM),
    )


def turned(factor_re, factor_im, value):
    return factor_re * value + factor_im * pltpu.roll(value, value.shape[-1] // 2, value.ndim - 1)


def product_call(norm, cols, energy, factors, panels, kinds, even_ends=None):
    steps = sum(part.shape[0] for part in energy)
    _, _, orbitals, depth = energy[0].shape
    width = 2 * orbitals
    runs = len(energy)
    shape = [jax.ShapeDtypeStruct((count, steps, orbitals, width), kind) for count, kind in kinds]
    places = [(n, at) for n, (count, _) in enumerate(kinds) for at in range(count)]
    pieces, tiles = len(panels), len(places)
    first = len(shape)
    if even_ends is None:
        shape.append(jax.ShapeDtypeStruct((tiles, orbitals, width), jnp.float32))
        extra = []
    else:
        shape += [
            jax.ShapeDtypeStruct((count, 2, orbitals, width), kind)
            for count, kind in ((3, jnp.bfloat16), (2, jnp.bfloat16), (3, jnp.float32))
        ]
        extra = [even_ends]
    packed = [(0, 0), (0, 1), (0, 2), (1, 0), (1, 1), (2, 0), (2, 1), (2, 2)]

    def body(cols_ref, *refs):
        energy_refs, (fre_ref, fim_ref), refs = refs[:runs], refs[runs : runs + 2], refs[runs + 2 :]
        even_refs, refs = refs[: len(extra)], refs[len(extra) :]
        panel_refs, out_refs = refs[: tiles * pieces], refs[tiles * pieces :]
        left = jnp.concatenate([ref[...].reshape(-1, depth) for ref in energy_refs], axis=0)
        right = jnp.concatenate(
            [
                jnp.concatenate(
                    [ref[...] for ref in panel_refs[tile * pieces : (tile + 1) * pieces]], axis=0
                )
                for tile in range(tiles)
            ],
            axis=1,
        )
        both = jnp.dot(left, right, preferred_element_type=jnp.float32)
        both = both.reshape(steps, 2, orbitals, tiles * width)
        lane = lax.broadcasted_iota(jnp.int32, (steps, orbitals, width), 2)
        sign = jnp.where(lane < orbitals, -norm, norm)
        for tile, (result, at) in enumerate(places):
            part_re = both[:, 0, :, tile * width : (tile + 1) * width]
            part_im = both[:, 1, :, tile * width : (tile + 1) * width]
            value = part_re * norm + sign * pltpu.roll(part_im, orbitals, 2)
            out_refs[result][at] = value.astype(kinds[result][1])
            end = jnp.zeros((orbitals, width), jnp.float32)
            for t in range(steps):
                end = turned(fre_ref[t], fim_ref[t], end + value[t])
            if not extra:
                out_refs[first][tile] = end
            else:
                group, place = packed[tile]
                target = out_refs[first + group]
                target[place, 0] = even_refs[0][tile].astype(target.dtype)
                target[place, 1] = end.astype(target.dtype)

    def panel_spec(panel, tile):
        return pl.BlockSpec((panel.shape[0], width), lambda n, cols: (0, cols[tile]))

    return pl.pallas_call(
        body,
        out_shape=shape,
        grid_spec=pltpu.PrefetchScalarGridSpec(
            num_scalar_prefetch=1,
            grid=(1,),
            in_specs=[pl.BlockSpec(memory_space=pltpu.VMEM)] * (runs + 2 + len(extra))
            + [panel_spec(panel, tile) for tile in range(tiles) for panel in panels],
            out_specs=[pl.BlockSpec(memory_space=pltpu.VMEM)] * len(shape),
        ),
        compiler_params=pltpu.CompilerParams(vmem_limit_bytes=34 << 20),
        cost_estimate=pl.CostEstimate(
            flops=2 * tiles * steps * 2 * orbitals * depth * width,
            bytes_accessed=2 * depth * (steps * 2 * orbitals + tiles * width),
            transcendentals=0,
        ),
    )(cols, *energy, *factors, *extra, *(panels * tiles))


def sum_kernel(own_ref, ahead_ref, back_ref, from5_ref, from3_ref, sum_ref):
    value = own_ref[0]
    for arrived in (ahead_ref[2], back_ref[1], from5_ref[...], from3_ref[...]):
        value = value + arrived.astype(jnp.float32)
    sum_ref[...] = value


def message_kernel(fre_ref, fim_ref, own_ref, ahead_ref, back_ref, from5_ref, from3_ref, msg_ref):
    steps, orbitals, width = fre_ref.shape
    lane = lax.broadcasted_iota(jnp.int32, (orbitals, width), 1)
    block = jnp.where(lane < width // 2, 1.0, 0.0).astype(jnp.float32)
    for t in range(steps):
        block = turned(fre_ref[t], fim_ref[t], block)
    for half in range(2):
        value = own_ref[0, half]
        for arrived in (ahead_ref[2, half], back_ref[1, half], from5_ref[half], from3_ref[half]):
            value = value + arrived.astype(jnp.float32)
        msg_ref[half] = value
    msg_ref[2] = block


def apply(later, earlier):
    width = later.shape[-1]
    lane = lax.broadcasted_iota(jnp.int32, later.shape[1:], 1)
    low = lane < width // 2
    factor = later[2]
    swapped = pltpu.roll(factor, width // 2, 1)
    fre = jnp.where(low, factor, swapped)
    fim = jnp.where(low, -swapped, factor)
    planes = [
        turned(fre, fim, earlier[0]) + later[0],
        turned(fre, fim, earlier[1]) + later[1],
        turned(fre, fim, earlier[2]),
    ]
    return planes


def chosen(keep, planes, other):
    return [jnp.where(keep, a, b) for a, b in zip(planes, other)]


def unit(shape):
    lane = lax.broadcasted_iota(jnp.int32, shape, 1)
    return [
        jnp.zeros(shape, jnp.float32),
        jnp.zeros(shape, jnp.float32),
        jnp.where(lane < shape[-1] // 2, 1.0, 0.0).astype(jnp.float32),
    ]


def read(ref):
    return [ref[0], ref[1], ref[2]]


class Planes:
    def __init__(self, planes):
        self.planes = planes
        self.shape = (3,) + planes[0].shape

    def __getitem__(self, index):
        return self.planes[index]


def after(later, earlier):
    return apply(Planes(later), Planes(earlier))


def chip_kernel(where_ref, own_ref, other_ref, out_ref):
    odd = where_ref[0] == 1
    own, other = read(own_ref), read(other_ref)
    later = chosen(odd, own, other)
    earlier = chosen(odd, other, own)
    for n, plane in enumerate(after(later, earlier)):
        out_ref[n] = plane


def before_of(at, behind, one):
    before = one
    for back in (3, 2, 1):
        here = chosen(at >= back, behind[back - 1], one)
        before = after(here, before)
    return before


def line_kernel(where_ref, own_ref, d1_ref, d2_ref, d3_ref, before_ref, total_ref):
    at = where_ref[1]
    one = unit(own_ref.shape[1:])
    behind = [read(d1_ref), read(d2_ref), read(d3_ref)]
    before = before_of(at, behind, one)
    for n, plane in enumerate(before):
        before_ref[n] = plane
    total = after(read(own_ref), before)
    for back in (3, 2, 1):
        here = chosen(at < back, behind[back - 1], one)
        total = after(here, total)
    for n, plane in enumerate(total):
        total_ref[n] = plane


def enter_kernel(where_ref, init_ref, d1_ref, d2_ref, d3_ref, x_ref, core_ref, out_ref):
    one = unit(init_ref.shape[1:])
    column = before_of(where_ref[2], [read(d1_ref), read(d2_ref), read(d3_ref)], one)
    start = after(column, [init_ref[0], init_ref[1], one[2]])
    start = after(read(x_ref), start)
    start = after(chosen(where_ref[0] == 1, read(core_ref), one), start)
    for half in range(2):
        out_ref[half] = start[half]


def last_kernel(
    fre_ref, fim_ref, enter_ref, even_ref, own_ref, ahead_ref, back_ref, from5_ref, from3_ref, out_ref
):
    steps = fre_ref.shape[0]
    even, odd = enter_ref[0], enter_ref[1]
    for t in range(steps):
        value = own_ref[0, t]
        for arrived in (ahead_ref[2, t], back_ref[1, t], from5_ref[t], from3_ref[t]):
            value = value + arrived.astype(jnp.float32)
        even = turned(fre_ref[t], fim_ref[t], even + even_ref[t])
        odd = turned(fre_ref[t], fim_ref[t], odd + value)
        out_ref[t, :, 0, :] = even
        out_ref[t, :, 1, :] = odd


def small_call(kernel, out_shape, scalars, *arrays):
    specs = [pl.BlockSpec(memory_space=pltpu.SMEM)] if scalars is not None else []
    specs += [pl.BlockSpec(memory_space=pltpu.VMEM)] * len(arrays)
    out_specs = jax.tree.map(lambda _: pl.BlockSpec(memory_space=pltpu.VMEM), out_shape)
    args = ([scalars] if scalars is not None else []) + list(arrays)
    return pl.pallas_call(
        kernel,
        out_shape=out_shape,
        in_specs=specs,
        out_specs=out_specs,
        compiler_params=pltpu.CompilerParams(vmem_limit_bytes=8 << 20),
        cost_estimate=pl.CostEstimate(flops=1000000, bytes_accessed=1 << 20, transcendentals=0),
    )(*args)


def near_line(local):
    moved = [local]
    for off in OFFSETS[1:]:
        moved.append(send(local, plane_perm(-off, True)))
    return [jnp.concatenate([m[chunk] for m in moved], axis=0) for chunk in range(2)]


def far_blocks(line):
    blocks = [line]
    for off in OFFSETS[1:]:
        blocks.append(send(line, plane_perm(-off, False)))
    return blocks


def add_rounded(*parts):
    total = parts[0]
    for part in parts[1:]:
        total = total + part.astype(jnp.float32)
    return total.astype(jnp.bfloat16)


SHARES = (4, 6, 1, 2, 7, 0, 3, 5)


def column_product(norm, cols_of, energy, factors, panels, even_ends=None):
    kinds = ((3, jnp.bfloat16), (2, jnp.bfloat16), (1, jnp.float32), (2, jnp.float32))
    return product_call(norm, cols_of(SHARES), energy, factors, panels, kinds, even_ends)


def column_sum(ahead, back, rest):
    ahead = send(ahead, depth_perm(1))
    back = send(back, depth_perm(-1))
    from5 = send(add_rounded(rest[1], ahead[1]), depth_perm(-3))
    from3 = send(add_rounded(rest[0], ahead[0], back[0]), depth_perm(3))
    return [ahead, back, from5, from3]


def slot_table(row_index):
    core = row_index % CORES
    x = (row_index // CORES) % X
    y = row_index // (CORES * X)
    offs = jnp.array(OFFSETS, jnp.int32)
    outer = jnp.repeat(offs, len(OFFSETS))
    inner = jnp.tile(offs, len(OFFSETS))

    def of(which):
        dy = jnp.where(which == 0, outer, inner)
        dx = jnp.where(which == 0, inner, outer)
        return (((y + dy) % Y) * X + (x + dx) % X) * CORES + which

    return jnp.concatenate([of(core), of(1 - core)]).astype(jnp.int32)


def per_device(retarded, mirrored, lesser_panel, initial, retention, phase_angle):
    row_index = lax.axis_index("row")
    col_index = lax.axis_index("col")
    steps, sources, orbitals, width = retarded.shape
    window = steps * lax.axis_size("row")
    panels = lesser_panel.shape[2]
    norm = 1.0 / (orbitals * math.sqrt(window))
    core = row_index % CORES
    x = (row_index // CORES) % X
    y = row_index // (CORES * X)
    where = jnp.stack([core, x, y]).astype(jnp.int32)
    way = jnp.where(core == 0, 1, -1)

    local = jnp.moveaxis(lesser_panel.reshape(orbitals, panels // 2, 2, width), 2, 0)
    local = local.reshape(2, orbitals, panels // 2 * width)
    times = jnp.stack([row_index * steps, col_index * sources]).astype(jnp.int32)
    slots = slot_table(row_index)
    energy = []
    for part in range(2):
        energy.append(energy_call(retarded, mirrored, slots, times, part, 2))

    def cols_of(rels):
        return ((col_index + way * jnp.array(rels, jnp.int32)) % Z).astype(jnp.int32)

    rotate_re = retention * jnp.cos(phase_angle)[None, :]
    rotate_im = retention * jnp.sin(phase_angle)[None, :]
    lane = jnp.arange(width, dtype=jnp.int32)
    sign = jnp.where(lane < orbitals, -1.0, 1.0).astype(jnp.float32)
    fre = jnp.broadcast_to(rotate_re[:, :, None], (steps, orbitals, width))
    fim = rotate_im[:, :, None] * sign
    start = jnp.swapaxes(initial, 0, 1)


    line0, line1 = near_line(local)
    blocks0 = far_blocks(line0)
    blocks1 = far_blocks(line1)
    panels0 = list(blocks0)
    for block in blocks0:
        panels0.append(send(block, CORE_SWAP))
    factors = (fre, fim)
    *terms0, own0, rest0, ends0 = column_product(norm, cols_of, energy, factors, panels0)
    parts0 = column_sum(*terms0, rest0)
    panels1 = list(blocks1)
    for block in blocks1:
        panels1.append(send(block, CORE_SWAP))
    *terms1, own1, rest1, ends_ahead, ends_back, ends_rest = column_product(
        norm, cols_of, energy, factors, panels1, ends0
    )
    end_parts = column_sum(ends_ahead, ends_back, ends_rest[1:])
    parts1 = column_sum(*terms1, rest1)

    message = jax.ShapeDtypeStruct((3, orbitals, width), jnp.float32)
    total = jax.ShapeDtypeStruct((steps, orbitals, width), jnp.float32)
    sum0 = small_call(sum_kernel, total, None, own0, *parts0)
    ends = small_call(message_kernel, message, None, fre, fim, ends_rest, *end_parts)
    other = send(ends, CORE_SWAP)
    chip = small_call(chip_kernel, message, where, ends, other)
    row_perm = lambda by: perm_of(lambda y, x, core, z: (y, x + by, core, z))
    column_perm = lambda by: perm_of(lambda y, x, core, z: (y + by, x, core, z))
    behind = [send(chip, row_perm(back)) for back in (1, 2, 3)]

    before_x, line = small_call(line_kernel, (message, message), where, chip, *behind)
    behind = [send(line, column_perm(back)) for back in (1, 2, 3)]
    entering = small_call(
        enter_kernel,
        jax.ShapeDtypeStruct((2, orbitals, width), jnp.float32),
        where,
        start,
        *behind,
        before_x,
        other,
    )
    return small_call(
        last_kernel,
        jax.ShapeDtypeStruct((steps, orbitals, 2, width), jnp.float32),
        None,
        fre,
        fim,
        entering,
        sum0,
        own1,
        *parts1,
    )


def solution(mesh):
    return jax.shard_map(
        per_device,
        mesh=mesh,
        in_specs=(
            P("row", "col", None, None),
            P("col", "row", None, None),
            P(("col", "row"), None, None, None),
            P(None, "col", None),
            P("row", None),
            P(),
        ),
        out_specs=P("row", None, "col", None),
        check_vma=False,
    )
```

```python
import math

import jax
import jax.numpy as jnp
from jax import lax
from jax.experimental import pallas as pl
from jax.experimental.pallas import tpu as pltpu
from jax.sharding import PartitionSpec as P


Y, X, CORES, Z = 4, 4, 2, 8
OFFSETS = (0, -1, 1, 2)
BOTH = ("row", "col")


def joint(y, x, core, z):
    return (((y % Y) * X + (x % X)) * CORES + core) * Z + z % Z


def perm_of(target):
    pairs = []
    for y in range(Y):
        for x in range(X):
            for core in range(CORES):
                for z in range(Z):
                    pairs.append((joint(y, x, core, z), joint(*target(y, x, core, z))))
    return pairs


def plane_perm(by, first):
    return perm_of(
        lambda y, x, core, z: (y, x + by, core, z)
        if (core == 0) == first
        else (y + by, x, core, z)
    )


def depth_perm(by):
    return perm_of(lambda y, x, core, z: (y, x, core, z + (by if core == 0 else -by)))


CORE_SWAP = perm_of(lambda y, x, core, z: (y, x, 1 - core, z))


def send(array, perm):
    return lax.ppermute(array, BOTH, perm)


def energy_kernel(skip, slots, times, ret_ref, mir_ref, out_ref):
    orbitals = ret_ref.shape[2]
    slot_count = ret_ref.shape[1]
    now = times[0] + skip + pl.program_id(0)
    first_source = times[1]
    low = lax.broadcasted_iota(jnp.int32, (orbitals, 2 * orbitals), 1) < orbitals
    low_row = lax.broadcasted_iota(jnp.int32, (1, 2 * orbitals), 1) < orbitals

    def pair(n, carry):
        s0 = slots[2 * n]
        s1 = slots[2 * n + 1]
        a0 = ret_ref[0, s0].astype(jnp.float32)
        a1 = ret_ref[0, s1].astype(jnp.float32)
        b = jnp.concatenate([mir_ref[s0, 0], mir_ref[s1, 0]], axis=0).astype(jnp.float32)
        keep0 = jnp.where(first_source + s0 <= now, 1.0, 0.0)
        keep1 = jnp.where(first_source + s1 <= now, 1.0, 0.0)
        keep = jnp.where(low_row, keep0, keep1)
        bt = b.T
        b_re = bt[:orbitals] * keep
        b_im = bt[orbitals:] * keep
        re = jnp.where(low, a0, pltpu.roll(a1, orbitals, 1))
        im = jnp.where(low, pltpu.roll(a0, orbitals, 1), a1)
        sq_re = re * re - im * im
        sq_im = 2.0 * re * im
        cols = pl.ds(pl.multiple_of(n * 2 * orbitals, 2 * orbitals), 2 * orbitals)
        out_ref[0, 0, :, cols] = (sq_re * b_re - sq_im * b_im).astype(jnp.bfloat16)
        out_ref[0, 1, :, cols] = (sq_re * b_im + sq_im * b_re).astype(jnp.bfloat16)
        return carry

    lax.fori_loop(0, slot_count // 2, pair, 0, unroll=4)


def energy_call(retarded, mirrored, slots, times, part, parts):
    steps, sources, orbitals, width = retarded.shape
    steps = steps // parts
    skip = part * steps
    return pl.pallas_call(
        lambda *refs: energy_kernel(skip, *refs),
        out_shape=jax.ShapeDtypeStruct((steps, 2, orbitals, sources * orbitals), jnp.bfloat16),
        grid_spec=pltpu.PrefetchScalarGridSpec(
            num_scalar_prefetch=2,
            grid=(steps,),
            in_specs=[
                pl.BlockSpec((1, sources, orbitals, width), lambda t, *_: (t + skip, 0, 0, 0)),
                pl.BlockSpec((sources, 1, orbitals, width), lambda t, *_: (0, t + skip, 0, 0)),
            ],
            out_specs=pl.BlockSpec(
                (1, 2, orbitals, sources * orbitals), lambda t, *_: (t, 0, 0, 0)
            ),
        ),
        compiler_params=pltpu.CompilerParams(vmem_limit_bytes=14 << 20),
        cost_estimate=pl.CostEstimate(
            flops=20 * steps * sources * orbitals * width,
            bytes_accessed=6 * steps * sources * orbitals * width,
            transcendentals=0,
        ),
    )(
        slots,
        times,
        pltpu.with_memory_space_constraint(retarded, pltpu.HBM),
        pltpu.with_memory_space_constraint(mirrored, pltpu.HBM),
    )


def turned(factor_re, factor_im, value):
    return factor_re * value + factor_im * pltpu.roll(value, value.shape[-1] // 2, value.ndim - 1)


def product_call(norm, cols, energy, factors, panels, kinds, even_ends=None):
    steps = sum(part.shape[0] for part in energy)
    _, _, orbitals, depth = energy[0].shape
    width = 2 * orbitals
    runs = len(energy)
    shape = [jax.ShapeDtypeStruct((count, steps, orbitals, width), kind) for count, kind in kinds]
    places = [(n, at) for n, (count, _) in enumerate(kinds) for at in range(count)]
    pieces, tiles = len(panels), len(places)
    first = len(shape)
    if even_ends is None:
        shape.append(jax.ShapeDtypeStruct((tiles, orbitals, width), jnp.float32))
        extra = []
    else:
        shape += [
            jax.ShapeDtypeStruct((count, 2, orbitals, width), kind)
            for count, kind in ((3, jnp.bfloat16), (2, jnp.bfloat16), (3, jnp.float32))
        ]
        extra = [even_ends]
    packed = [(0, 0), (0, 1), (0, 2), (1, 0), (1, 1), (2, 0), (2, 1), (2, 2)]

    def body(cols_ref, *refs):
        energy_refs, (fre_ref, fim_ref), refs = refs[:runs], refs[runs : runs + 2], refs[runs + 2 :]
        even_refs, refs = refs[: len(extra)], refs[len(extra) :]
        panel_refs, out_refs = refs[:pieces], refs[pieces:]
        starts = [pl.multiple_of(cols_ref[tile] * width, width) for tile in range(tiles)]
        left = jnp.concatenate([ref[...].reshape(-1, depth) for ref in energy_refs], axis=0)
        right = jnp.concatenate(
            [
                jnp.concatenate([ref[:, pl.ds(starts[tile], width)] for ref in panel_refs], axis=0)
                for tile in range(tiles)
            ],
            axis=1,
        )
        both = jnp.dot(left, right, preferred_element_type=jnp.float32)
        both = both.reshape(steps, 2, orbitals, tiles * width)
        lane = lax.broadcasted_iota(jnp.int32, (steps, orbitals, width), 2)
        sign = jnp.where(lane < orbitals, -norm, norm)
        for tile, (result, at) in enumerate(places):
            part_re = both[:, 0, :, tile * width : (tile + 1) * width]
            part_im = both[:, 1, :, tile * width : (tile + 1) * width]
            value = part_re * norm + sign * pltpu.roll(part_im, orbitals, 2)
            out_refs[result][at] = value.astype(kinds[result][1])
            end = jnp.zeros((orbitals, width), jnp.float32)
            for t in range(steps):
                end = turned(fre_ref[t], fim_ref[t], end + value[t])
            if not extra:
                out_refs[first][tile] = end
            else:
                group, place = packed[tile]
                target = out_refs[first + group]
                target[place, 0] = even_refs[0][tile].astype(target.dtype)
                target[place, 1] = end.astype(target.dtype)

    vmem = pl.BlockSpec(memory_space=pltpu.VMEM)
    return pl.pallas_call(
        body,
        out_shape=shape,
        in_specs=[pl.BlockSpec(memory_space=pltpu.SMEM)] + [vmem] * (runs + 2 + len(extra) + pieces),
        out_specs=[vmem] * len(shape),
        compiler_params=pltpu.CompilerParams(vmem_limit_bytes=34 << 20),
        cost_estimate=pl.CostEstimate(
            flops=2 * tiles * steps * 2 * orbitals * depth * width,
            bytes_accessed=2 * depth * (steps * 2 * orbitals + tiles * width),
            transcendentals=0,
        ),
    )(cols, *energy, *factors, *extra, *panels)


def sum_kernel(own_ref, ahead_ref, back_ref, from5_ref, from3_ref, sum_ref):
    value = own_ref[0]
    for arrived in (ahead_ref[2], back_ref[1], from5_ref[...], from3_ref[...]):
        value = value + arrived.astype(jnp.float32)
    sum_ref[...] = value


def message_kernel(fre_ref, fim_ref, own_ref, ahead_ref, back_ref, from5_ref, from3_ref, msg_ref):
    steps, orbitals, width = fre_ref.shape
    lane = lax.broadcasted_iota(jnp.int32, (orbitals, width), 1)
    block = jnp.where(lane < width // 2, 1.0, 0.0).astype(jnp.float32)
    for t in range(steps):
        block = turned(fre_ref[t], fim_ref[t], block)
    for half in range(2):
        value = own_ref[0, half]
        for arrived in (ahead_ref[2, half], back_ref[1, half], from5_ref[half], from3_ref[half]):
            value = value + arrived.astype(jnp.float32)
        msg_ref[half] = value
    msg_ref[2] = block


def apply(later, earlier):
    width = later.shape[-1]
    lane = lax.broadcasted_iota(jnp.int32, later.shape[1:], 1)
    low = lane < width // 2
    factor = later[2]
    swapped = pltpu.roll(factor, width // 2, 1)
    fre = jnp.where(low, factor, swapped)
    fim = jnp.where(low, -swapped, factor)
    planes = [
        turned(fre, fim, earlier[0]) + later[0],
        turned(fre, fim, earlier[1]) + later[1],
        turned(fre, fim, earlier[2]),
    ]
    return planes


def chosen(keep, planes, other):
    return [jnp.where(keep, a, b) for a, b in zip(planes, other)]


def unit(shape):
    lane = lax.broadcasted_iota(jnp.int32, shape, 1)
    return [
        jnp.zeros(shape, jnp.float32),
        jnp.zeros(shape, jnp.float32),
        jnp.where(lane < shape[-1] // 2, 1.0, 0.0).astype(jnp.float32),
    ]


def read(ref):
    return [ref[0], ref[1], ref[2]]


class Planes:
    def __init__(self, planes):
        self.planes = planes
        self.shape = (3,) + planes[0].shape

    def __getitem__(self, index):
        return self.planes[index]


def after(later, earlier):
    return apply(Planes(later), Planes(earlier))


def chip_kernel(where_ref, own_ref, other_ref, out_ref):
    odd = where_ref[0] == 1
    own, other = read(own_ref), read(other_ref)
    later = chosen(odd, own, other)
    earlier = chosen(odd, other, own)
    for n, plane in enumerate(after(later, earlier)):
        out_ref[n] = plane


def before_of(at, behind, one):
    before = one
    for back in (3, 2, 1):
        here = chosen(at >= back, behind[back - 1], one)
        before = after(here, before)
    return before


def line_kernel(where_ref, own_ref, d1_ref, d2_ref, d3_ref, before_ref, total_ref):
    at = where_ref[1]
    one = unit(own_ref.shape[1:])
    behind = [read(d1_ref), read(d2_ref), read(d3_ref)]
    before = before_of(at, behind, one)
    for n, plane in enumerate(before):
        before_ref[n] = plane
    total = after(read(own_ref), before)
    for back in (3, 2, 1):
        here = chosen(at < back, behind[back - 1], one)
        total = after(here, total)
    for n, plane in enumerate(total):
        total_ref[n] = plane


def last_kernel(
    where_ref,
    fre_ref,
    fim_ref,
    init_ref,
    d1_ref,
    d2_ref,
    d3_ref,
    x_ref,
    core_ref,
    even_ref,
    own_ref,
    ahead_ref,
    back_ref,
    from5_ref,
    from3_ref,
    out_ref,
):
    steps = fre_ref.shape[0]
    one = unit(init_ref.shape[1:])
    column = before_of(where_ref[2], [read(d1_ref), read(d2_ref), read(d3_ref)], one)
    start = after(column, [init_ref[0], init_ref[1], one[2]])
    start = after(read(x_ref), start)
    start = after(chosen(where_ref[0] == 1, read(core_ref), one), start)
    even, odd = start[0], start[1]
    for t in range(steps):
        value = own_ref[0, t]
        for arrived in (ahead_ref[2, t], back_ref[1, t], from5_ref[t], from3_ref[t]):
            value = value + arrived.astype(jnp.float32)
        even = turned(fre_ref[t], fim_ref[t], even + even_ref[t])
        odd = turned(fre_ref[t], fim_ref[t], odd + value)
        out_ref[t, :, 0, :] = even
        out_ref[t, :, 1, :] = odd


def small_call(kernel, out_shape, scalars, *arrays):
    specs = [pl.BlockSpec(memory_space=pltpu.SMEM)] if scalars is not None else []
    specs += [pl.BlockSpec(memory_space=pltpu.VMEM)] * len(arrays)
    out_specs = jax.tree.map(lambda _: pl.BlockSpec(memory_space=pltpu.VMEM), out_shape)
    args = ([scalars] if scalars is not None else []) + list(arrays)
    return pl.pallas_call(
        kernel,
        out_shape=out_shape,
        in_specs=specs,
        out_specs=out_specs,
        compiler_params=pltpu.CompilerParams(vmem_limit_bytes=8 << 20),
        cost_estimate=pl.CostEstimate(flops=1000000, bytes_accessed=1 << 20, transcendentals=0),
    )(*args)


def near_line(local):
    moved = [local]
    for off in OFFSETS[1:]:
        moved.append(send(local, plane_perm(-off, True)))
    return [jnp.concatenate([m[chunk] for m in moved], axis=0) for chunk in range(2)]


def far_blocks(line):
    blocks = [line]
    for off in OFFSETS[1:]:
        blocks.append(send(line, plane_perm(-off, False)))
    return blocks


def add_rounded(*parts):
    total = parts[0]
    for part in parts[1:]:
        total = total + part.astype(jnp.float32)
    return total.astype(jnp.bfloat16)


SHARES = (4, 6, 1, 2, 7, 0, 3, 5)


def column_product(norm, cols_of, energy, factors, panels, even_ends=None):
    kinds = ((3, jnp.bfloat16), (2, jnp.bfloat16), (1, jnp.float32), (2, jnp.float32))
    return product_call(norm, cols_of(SHARES), energy, factors, panels, kinds, even_ends)


def column_sum(ahead, back, rest):
    ahead = send(ahead, depth_perm(1))
    back = send(back, depth_perm(-1))
    from5 = send(add_rounded(rest[1], ahead[1]), depth_perm(-3))
    from3 = send(add_rounded(rest[0], ahead[0], back[0]), depth_perm(3))
    return [ahead, back, from5, from3]


def slot_table(row_index):
    core = row_index % CORES
    x = (row_index // CORES) % X
    y = row_index // (CORES * X)
    offs = jnp.array(OFFSETS, jnp.int32)
    outer = jnp.repeat(offs, len(OFFSETS))
    inner = jnp.tile(offs, len(OFFSETS))

    def of(which):
        dy = jnp.where(which == 0, outer, inner)
        dx = jnp.where(which == 0, inner, outer)
        return (((y + dy) % Y) * X + (x + dx) % X) * CORES + which

    return jnp.concatenate([of(core), of(1 - core)]).astype(jnp.int32)


def per_device(retarded, mirrored, lesser_panel, initial, retention, phase_angle):
    row_index = lax.axis_index("row")
    col_index = lax.axis_index("col")
    steps, sources, orbitals, width = retarded.shape
    window = steps * lax.axis_size("row")
    panels = lesser_panel.shape[2]
    norm = 1.0 / (orbitals * math.sqrt(window))
    core = row_index % CORES
    x = (row_index // CORES) % X
    y = row_index // (CORES * X)
    where = jnp.stack([core, x, y]).astype(jnp.int32)
    way = jnp.where(core == 0, 1, -1)

    local = jnp.moveaxis(lesser_panel.reshape(orbitals, panels // 2, 2, width), 2, 0)
    local = local.reshape(2, orbitals, panels // 2 * width)
    times = jnp.stack([row_index * steps, col_index * sources]).astype(jnp.int32)
    slots = slot_table(row_index)
    energy = []
    for part in range(2):
        energy.append(energy_call(retarded, mirrored, slots, times, part, 2))

    def cols_of(rels):
        return ((col_index + way * jnp.array(rels, jnp.int32)) % Z).astype(jnp.int32)

    rotate_re = retention * jnp.cos(phase_angle)[None, :]
    rotate_im = retention * jnp.sin(phase_angle)[None, :]
    lane = jnp.arange(width, dtype=jnp.int32)
    sign = jnp.where(lane < orbitals, -1.0, 1.0).astype(jnp.float32)
    fre = jnp.broadcast_to(rotate_re[:, :, None], (steps, orbitals, width))
    fim = rotate_im[:, :, None] * sign
    start = jnp.swapaxes(initial, 0, 1)


    line0, line1 = near_line(local)
    blocks0 = far_blocks(line0)
    blocks1 = far_blocks(line1)
    panels0 = list(blocks0)
    for block in blocks0:
        panels0.append(send(block, CORE_SWAP))
    factors = (fre, fim)
    *terms0, own0, rest0, ends0 = column_product(norm, cols_of, energy, factors, panels0)
    parts0 = column_sum(*terms0, rest0)
    panels1 = list(blocks1)
    for block in blocks1:
        panels1.append(send(block, CORE_SWAP))
    *terms1, own1, rest1, ends_ahead, ends_back, ends_rest = column_product(
        norm, cols_of, energy, factors, panels1, ends0
    )
    end_parts = column_sum(ends_ahead, ends_back, ends_rest[1:])
    parts1 = column_sum(*terms1, rest1)

    message = jax.ShapeDtypeStruct((3, orbitals, width), jnp.float32)
    total = jax.ShapeDtypeStruct((steps, orbitals, width), jnp.float32)
    sum0 = small_call(sum_kernel, total, None, own0, *parts0)
    ends = small_call(message_kernel, message, None, fre, fim, ends_rest, *end_parts)
    other = send(ends, CORE_SWAP)
    chip = small_call(chip_kernel, message, where, ends, other)
    row_perm = lambda by: perm_of(lambda y, x, core, z: (y, x + by, core, z))
    column_perm = lambda by: perm_of(lambda y, x, core, z: (y + by, x, core, z))
    behind = [send(chip, row_perm(back)) for back in (1, 2, 3)]

    before_x, line = small_call(line_kernel, (message, message), where, chip, *behind)
    behind = [send(line, column_perm(back)) for back in (1, 2, 3)]
    return small_call(
        last_kernel,
        jax.ShapeDtypeStruct((steps, orbitals, 2, width), jnp.float32),
        where,
        fre,
        fim,
        start,
        *behind,
        before_x,
        other,
        sum0,
        own1,
        *parts1,
    )


def solution(mesh):
    return jax.shard_map(
        per_device,
        mesh=mesh,
        in_specs=(
            P("row", "col", None, None),
            P("col", "row", None, None),
            P(("col", "row"), None, None, None),
            P(None, "col", None),
            P("row", None),
            P(),
        ),
        out_specs=P("row", None, "col", None),
        check_vma=False,
    )
```
